256 devices in a mesh: section: 16 (over y_hi, z), fsdp: 16 (over x, y_lo, core).
Axes of the slice: x: 4, y: 4 (y_hi: 2, y_lo: 2; y = y_hi * 2 + y_lo), z: 8, core: 2. Of those that a mesh axis runs over, the one named last changes fastest.
Arguments:
- branch_in: bfloat16 [16, 8192, 128], P('section', 'fsdp'), may hold values from -0.0625 to 0.0625
- branch_out: bfloat16 [16, 128, 8192], P('section', None, 'fsdp'), may hold values from -0.5 to 0.5
- down_inputs: bfloat16 [16, 12, 128, 8192], P('section', None, 'fsdp'), may hold values from -6 to 6
- up_inputs: bfloat16 [16, 12, 128, 8192], P('section', None, 'fsdp'), may hold values from -6 to 6
- top_grads: bfloat16 [2, 12, 128, 8192], P(None, None, 'fsdp'), may hold values from -6 to 6
- plan: int32 [2, 12], replicated, may hold values from 0 to 11, each once within a row
- reward_pos: int32 [2, 12, 16], replicated, may hold values from 0 to 7
- reward_cot: float32 [2, 12, 16], replicated, may hold values from -4 to 4
- reward_head: float32 [8192], replicated, may hold values from -5 to 5
Outputs:
- grad_in: float32 [16, 8192, 128], P('section', 'fsdp')
- grad_out: float32 [16, 128, 8192], P('section', None, 'fsdp')
The draws below stay inside these ranges and needn't reach their ends.
Inputs may be any that keep to these rules, and one draw needn't show every extreme that they name: Each row of plan names every microbatch once.
All inputs are finite; a program needn't handle non-finite values.
Results may differ from the reference program's by a relative error of at most 0.03.
Values may be sent and summed in bfloat16 or wider, within the bound.
No kernel may reach another device: no remote copies, remote signals or barrier semaphores. Data moves between devices by JAX's collectives and lax.ppermute only.
A program may use at most 128 MiB of HBM per device.

```python
import jax
import jax.numpy as jnp
from jax import lax

D = 8192
R = 128
ROWS = 8
MICRO = 12
SEQS = 16
LAYERS = 16
TOK = 128
SEQ_LEN = 8
N_FSDP = 16


def touch_ends(drawn, own_key, smallest, largest):
    spot = [jax.random.randint(jax.random.fold_in(own_key, axis), (), 0, length) for axis, length in enumerate(drawn.shape)]
    widest = drawn.shape.index(max(drawn.shape))
    neighbour = spot[:widest] + [(spot[widest] + 1) % drawn.shape[widest]] + spot[widest + 1:]
    return drawn.at[tuple(spot)].set(smallest).at[tuple(neighbour)].set(largest)


def levels(stream_key, shape, shards, low, high):
    gain = 1.0
    for axis_at, shards_of in shards:
        steps = jax.random.uniform(jax.random.fold_in(jax.random.fold_in(stream_key, 6), axis_at), (shards_of,), jnp.float32, low / len(shards), high / len(shards))
        gain = gain * jnp.repeat(jnp.exp(steps), shape[axis_at] // shards_of).reshape((-1,) + (1,) * (len(shape) - 1 - axis_at))
    return gain


def centred(own_key, shape, width, limit, split=(), kind=jnp.bfloat16):
    drawn = jax.random.normal(own_key, shape, jnp.float32) * width
    if len(split) > 0:
        drawn = levels(own_key, shape, split, -0.22, 0.18) * drawn
    return jnp.clip(drawn, min=-limit, max=limit).astype(kind)


def setup_inputs(seed: int = 0) -> dict:
    keys = jax.random.split(jax.random.key(seed), 10)
    branch_in = centred(keys[0], (LAYERS, D, R), D ** -0.5, 0.0625, ((0, 16), (1, 16)))
    branch_out = centred(keys[1], (LAYERS, R, D), R ** -0.5, 0.5, ((0, 16), (2, 16)))
    down_inputs = centred(keys[2], (LAYERS, MICRO, TOK, D), 1.0, 6.0, ((0, 16), (2, 16)))
    up_inputs = centred(keys[3], (LAYERS, MICRO, TOK, D), 1.0, 6.0, ((0, 16), (2, 16)))
    top_grads = centred(keys[4], (2, MICRO, TOK, D), 1.0, 6.0, ((2, 16),))
    plan = jax.vmap(lambda own: jax.random.permutation(own, MICRO))(jax.random.split(keys[5], 2)).reshape((2, MICRO)).astype(jnp.int32)
    reward_pos = touch_ends(jax.random.randint(keys[6], (2, MICRO, SEQS), 0, SEQ_LEN), jax.random.fold_in(keys[6], 1), 0, SEQ_LEN - 1).astype(jnp.int32)
    reward_cot = centred(keys[7], (2, MICRO, SEQS), 1.0, 4.0, (), jnp.float32)
    reward_head = centred(keys[8], (D,), 1.0, 5.0, (), jnp.float32)
    return {"branch_in": branch_in, "branch_out": branch_out, "down_inputs": down_inputs, "up_inputs": up_inputs, "top_grads": top_grads, "plan": plan, "reward_pos": reward_pos, "reward_cot": reward_cot, "reward_head": reward_head}


def branch_grads(inputs, grad, w_in, w_out):
    pre_act = jnp.dot(inputs, w_in, preferred_element_type=jnp.float32)
    sig_val = jax.nn.sigmoid(pre_act)
    hidden = (pre_act * sig_val).astype(jnp.bfloat16)
    grad_hidden = lax.dot_general(grad, w_out, (((1,), (1,)), ((), ())), preferred_element_type=jnp.float32)
    grad_pre = (grad_hidden * sig_val * (1.0 + pre_act * (1.0 - sig_val))).astype(jnp.bfloat16)
    back_term = lax.dot_general(grad_pre, w_in, (((1,), (1,)), ((), ())), preferred_element_type=jnp.float32)
    back = (grad.astype(jnp.float32) + back_term).astype(jnp.bfloat16)
    return hidden, grad_pre, back


def block_sums(inputs, hidden, grad, grad_pre):
    in_blocks = inputs.reshape(MICRO, N_FSDP, ROWS, D).astype(jnp.float32)
    hid_blocks = hidden.reshape(MICRO, N_FSDP, ROWS, R).astype(jnp.float32)
    grad_blocks = grad.reshape(MICRO, N_FSDP, ROWS, D).astype(jnp.float32)
    pre_blocks = grad_pre.reshape(MICRO, N_FSDP, ROWS, R).astype(jnp.float32)
    part_in = jnp.einsum('mfrd,mfrk->fdk', in_blocks, pre_blocks)
    part_out = jnp.einsum('mfrk,mfrd->fkd', hid_blocks, grad_blocks)
    part_in = part_in.astype(jnp.bfloat16).astype(jnp.float32)
    part_out = part_out.astype(jnp.bfloat16).astype(jnp.float32)
    return jnp.sum(part_in, axis=0), jnp.sum(part_out, axis=0)


def layer_step(grad, pieces):
    inputs, w_in, w_out = pieces
    flat_in = inputs.reshape(MICRO * TOK, D)
    flat_grad = grad.reshape(MICRO * TOK, D)
    hidden, grad_pre, back = branch_grads(flat_in, flat_grad, w_in, w_out)
    part_in, part_out = block_sums(flat_in, hidden, flat_grad, grad_pre)
    back = back.reshape(MICRO, TOK, D)
    return back, (part_in, part_out)


def first_gradient(top, order, positions, rewards, head):
    placed = jnp.zeros_like(top).at[order].set(top)
    target = jnp.arange(SEQS, dtype=jnp.int32)[None, :] * SEQ_LEN + positions
    match = target[:, :, None] == jnp.arange(TOK, dtype=jnp.int32)[None, None, :]
    row_weight = jnp.sum(jnp.where(match, rewards[:, :, None], jnp.zeros((), jnp.float32)), axis=1)
    total = placed.astype(jnp.float32) + row_weight[:, :, None] * head[None, None, :]
    return total.astype(jnp.bfloat16)


def reference(branch_in, branch_out, down_inputs, up_inputs, top_grads, plan, reward_pos, reward_cot, reward_head):
    first_down = first_gradient(top_grads[0], plan[0], reward_pos[0], reward_cot[0], reward_head)
    first_up = first_gradient(top_grads[1], plan[1], reward_pos[1], reward_cot[1], reward_head)
    _, (down_in, down_out) = lax.scan(layer_step, first_down, (down_inputs[::-1], branch_in[::-1], branch_out[::-1]))
    _, (up_in, up_out) = lax.scan(layer_step, first_up, (up_inputs, branch_in[::-1], branch_out[::-1]))
    grad_in = down_in[::-1] + up_in[::-1]
    grad_out = down_out[::-1] + up_out[::-1]
    return grad_in, grad_out
```

```python
import jax
import jax.numpy as jnp
from jax import lax
from jax.experimental import pallas as pl
from jax.experimental.pallas import tpu as pltpu
from jax.sharding import PartitionSpec as P

BF16 = jnp.bfloat16
F32 = jnp.float32
ROWS_OF_BOTH = (((0,), (0,)), ((), ()))
COLS_OF_BOTH = (((1,), (1,)), ((), ()))


def dot(left, right, dims=(((1,), (0,)), ((), ()))):
    return lax.dot_general(left, right, dims, preferred_element_type=F32)


def from_above(value, steps):
    count = lax.axis_size("section")
    return lax.ppermute(value, "section", [((k + steps) % count, k) for k in range(count)])


def mirrored(value):
    count = lax.axis_size("section")
    return lax.ppermute(value, "section", [(k, count - 1 - k) for k in range(count)])


def exchanged(parts, axis):
    return lax.all_to_all(parts, axis, 0, 0, tiled=True)


def spread(value, axis):
    return exchanged(jnp.broadcast_to(value[None], (lax.axis_size(axis),) + value.shape), axis)


def vmem():
    return pl.BlockSpec(memory_space=pltpu.VMEM)


def smem():
    return pl.BlockSpec(memory_space=pltpu.SMEM)


def couplings(section, in_t, out_t, near, count):
    units = in_t.shape[0]
    slots = len(near)

    def kernel(section_ref, in_ref, out_ref, *refs):
        dest = refs[slots]
        for slot in range(slots):
            wrapped = section_ref[0] + slot + 1 >= count

            @pl.when(wrapped)
            def _():
                dest[slot] = dot(in_ref[...], refs[slot][...], COLS_OF_BOTH).astype(BF16)

            @pl.when(jnp.logical_not(wrapped))
            def _():
                dest[slot] = dot(refs[slot][...], out_ref[...], COLS_OF_BOTH).astype(BF16)

    return pl.pallas_call(
        kernel,
        out_shape=jax.ShapeDtypeStruct((slots, units, units), BF16),
        in_specs=[smem()] + [vmem()] * (2 + slots),
        out_specs=vmem(),
        name="couplings",
    )(section, in_t, out_t, *near)


def pre_parts(wide, in_t, far_in_t, step):
    blocks, rows, part = wide.shape
    units = in_t.shape[0]
    half = rows // 2

    def kernel(wide_ref, in_ref, far_ref, dest):
        for b in range(step):
            dest[b, :half] = dot(wide_ref[b, :half], in_ref[...], COLS_OF_BOTH).astype(BF16)
            dest[b, half:] = dot(wide_ref[b, half:], far_ref[...], COLS_OF_BOTH).astype(BF16)

    return pl.pallas_call(
        kernel,
        grid=(blocks // step,),
        out_shape=jax.ShapeDtypeStruct((blocks, rows, units), BF16),
        in_specs=[
            pl.BlockSpec((step, rows, part), lambda b: (b, 0, 0)),
            pl.BlockSpec((units, part), lambda b: (0, 0)),
            pl.BlockSpec((units, part), lambda b: (0, 0)),
        ],
        out_specs=pl.BlockSpec((step, rows, units), lambda b: (b, 0, 0)),
        name="pre_parts",
    )(wide, in_t, far_in_t)


def top_products(top, row_weight, head, out_full, place, step):
    blocks, units, part = out_full.shape
    rows = top.shape[0]

    def kernel(top_ref, weight_ref, head_ref, out_ref, place_ref, dest, acc):
        at = pl.program_id(0)

        @pl.when(at == 0)
        def _():
            acc[...] = jnp.zeros_like(acc)

        first = (top_ref[...].astype(F32) + weight_ref[...] * head_ref[...]).astype(BF16)
        total = acc[...]
        for b in range(step):
            total = total + dot(first[:, b * part : (b + 1) * part], out_ref[b], COLS_OF_BOTH)
        acc[...] = total

        @pl.when(at == pl.num_programs(0) - 1)
        def _():
            dest[...] = dot(place_ref[...], acc[...].astype(BF16)).astype(BF16)

    return pl.pallas_call(
        kernel,
        grid=(blocks // step,),
        out_shape=jax.ShapeDtypeStruct((rows, units), BF16),
        in_specs=[
            pl.BlockSpec((rows, step * part), lambda b: (0, b)),
            pl.BlockSpec((rows, 1), lambda b: (0, 0)),
            pl.BlockSpec((1, step * part), lambda b: (0, b)),
            pl.BlockSpec((step, units, part), lambda b: (b, 0, 0)),
            pl.BlockSpec((rows, rows), lambda b: (0, 0)),
        ],
        out_specs=pl.BlockSpec((rows, units), lambda b: (0, 0)),
        scratch_shapes=[pltpu.VMEM((rows, units), F32)],
        name="top_products",
    )(top, row_weight, head, out_full, place)


def first_parts(top, row_weight, head, pre, place, blocks, step):
    rows, width = top.shape
    units = pre.shape[1]
    part = width // blocks

    def kernel(top_ref, weight_ref, head_ref, pre_ref, place_ref, dest):
        value = pre_ref[...].astype(F32)
        hidden = (value * jax.nn.sigmoid(value)).astype(BF16)
        placed = dot(hidden, place_ref[...], ROWS_OF_BOTH).astype(BF16)
        first = (top_ref[...].astype(F32) + weight_ref[...] * head_ref[...]).astype(BF16)
        total = dot(placed, first).astype(BF16)
        for b in range(step):
            dest[b] = total[:, b * part : (b + 1) * part]

    return pl.pallas_call(
        kernel,
        grid=(blocks // step,),
        out_shape=jax.ShapeDtypeStruct((blocks, units, part), BF16),
        in_specs=[
            pl.BlockSpec((rows, step * part), lambda b: (0, b)),
            pl.BlockSpec((rows, 1), lambda b: (0, 0)),
            pl.BlockSpec((1, step * part), lambda b: (0, b)),
            pl.BlockSpec((rows, units), lambda b: (0, 0)),
            pl.BlockSpec((rows, rows), lambda b: (0, 0)),
        ],
        out_specs=pl.BlockSpec((step, units, part), lambda b: (b, 0, 0)),
        name="first_parts",
    )(top, row_weight, head, pre, place)


def chain(section, known, coupled):
    count, tall, units = known.shape
    rows = tall // 2
    half = rows // 2
    blocks, _, piece, _ = coupled.shape
    pieces = units // piece

    def kernel(section_ref, known_ref, coupled_ref, dest, reach, grads):
        def pre_of(layer, other):
            return jnp.concatenate(
                [known_ref[layer, :half], known_ref[other, half:rows]], axis=0
            ).astype(F32)

        def coupling(upper, lower):
            gap = upper - lower
            if gap <= count // 2:
                at, slot = lower, gap - 1
            else:
                at, slot = upper, count - gap - 1
            return jnp.concatenate(
                [coupled_ref[slot * pieces + p, at] for p in range(pieces)], axis=0
            )

        for layer in range(count):
            reach[layer] = known_ref[layer, rows:].astype(F32)
        for layer in range(count - 1, -1, -1):
            pre = pre_of(layer, count - 1 - layer)
            sig = jax.nn.sigmoid(pre)
            grad_pre = (reach[layer] * sig * (1.0 + pre * (1.0 - sig))).astype(BF16)
            grads[layer] = grad_pre
            if layer > 0:
                lower = jnp.concatenate([coupling(layer, low) for low in range(layer)], axis=1)
                update = dot(grad_pre, lower)
                for low in range(layer):
                    reach[low] += update[:, low * units : (low + 1) * units]
        own = section_ref[0]
        far = count - 1 - own
        pre = pre_of(own, far)
        hidden = (pre * jax.nn.sigmoid(pre)).astype(BF16)
        above = jnp.concatenate(
            [grads[jnp.minimum(own + up, count - 1)] for up in range(1, count)], axis=1
        )
        cross = dot(hidden, above, ROWS_OF_BOTH)
        sent = jnp.concatenate([grads[own][:half], grads[far][half:]], axis=0)
        for up in range(count):
            if up == 0:
                dest[up, :units] = jnp.zeros((units, units), BF16)
            else:
                block = cross[:, (up - 1) * units : up * units]
                dest[up, :units] = jnp.where(own + up < count, block, 0.0).astype(BF16)
            dest[up, units:] = sent

    return pl.pallas_call(
        kernel,
        out_shape=jax.ShapeDtypeStruct((count, units + rows, units), BF16),
        in_specs=[smem(), vmem(), vmem()],
        out_specs=vmem(),
        scratch_shapes=[pltpu.VMEM((count, rows, units), F32), pltpu.VMEM((count, rows, units), BF16)],
        name="chain",
    )(section, known, coupled)


def input_grads(wide, shared, step):
    blocks, rows, part = wide.shape
    tall, units = shared.shape[1:]
    half = rows // 2
    skip = tall - rows

    def kernel(wide_ref, shared_ref, own, far, own_acc, far_acc):
        at = pl.program_id(0)

        @pl.when(at == 0)
        def _():
            own_acc[...] = jnp.zeros_like(own_acc)
            far_acc[...] = jnp.zeros_like(far_acc)

        for b in range(step):
            own_acc[...] += dot(
                shared_ref[b, skip : skip + half], wide_ref[b, :half], ROWS_OF_BOTH
            )
            far_acc[...] += dot(shared_ref[b, skip + half :], wide_ref[b, half:], ROWS_OF_BOTH)

        @pl.when(at == pl.num_programs(0) - 1)
        def _():
            own[...] = own_acc[...]
            far[...] = far_acc[...].astype(BF16)

    return pl.pallas_call(
        kernel,
        grid=(blocks // step,),
        out_shape=[
            jax.ShapeDtypeStruct((units, part), F32),
            jax.ShapeDtypeStruct((units, part), BF16),
        ],
        in_specs=[
            pl.BlockSpec((step, rows, part), lambda b: (b, 0, 0)),
            pl.BlockSpec((step, tall, units), lambda b: (b, 0, 0)),
        ],
        out_specs=[
            pl.BlockSpec((units, part), lambda b: (0, 0)),
            pl.BlockSpec((units, part), lambda b: (0, 0)),
        ],
        scratch_shapes=[pltpu.VMEM((units, part), F32), pltpu.VMEM((units, part), F32)],
        name="input_grads",
    )(wide, shared)


def output_grads(cross, firsts, near, far):
    count, units, _ = cross.shape
    blocks, _, part = firsts.shape
    slots = len(near)

    def kernel(cross_ref, first_ref, far_ref, *refs):
        dest = refs[slots]
        total = jnp.zeros((units, part), F32)
        for b in range(blocks):
            total = total + first_ref[b].astype(F32)
        for up in range(1, count):
            other = refs[up - 1][...] if up <= slots else far_ref[up - 1 - slots]
            total = total + dot(cross_ref[up], other)
        dest[...] = total

    return pl.pallas_call(
        kernel,
        out_shape=jax.ShapeDtypeStruct((units, part), F32),
        in_specs=[vmem()] * (3 + slots),
        out_specs=vmem(),
        name="output_grads",
    )(cross, firsts, far, *near)


def on_device(
    branch_in,
    branch_out,
    down_inputs,
    up_inputs,
    top_grads,
    plan,
    reward_pos,
    reward_cot,
    reward_head,
):
    count = lax.axis_size("section")
    blocks = lax.axis_size("fsdp")
    section_idx = lax.axis_index("section")
    fsdp_idx = lax.axis_index("fsdp")
    section = section_idx.astype(jnp.int32).reshape(1)
    _, micro, row_count, width = down_inputs.shape
    units = branch_in.shape[2]
    part = width // blocks
    half = micro * row_count
    rows = 2 * half
    step = 4

    in_t = branch_in[0].T
    out_t = branch_out[0]
    near = [
        from_above(jnp.where(section_idx >= up, in_t, out_t), up) for up in range(1, count // 2 + 1)
    ]
    far_in_t = mirrored(in_t)
    out_full = lax.all_gather(out_t, "fsdp", axis=0)

    narrow = jnp.concatenate(
        [down_inputs[0].reshape(half, width), up_inputs[0].reshape(half, width)], axis=0
    )
    wide = exchanged(jnp.transpose(narrow.reshape(rows, blocks, part), (1, 0, 2)), "fsdp")

    coupled = couplings(section, in_t, out_t, near, count)
    coupled = exchanged(coupled.reshape(blocks, -1, units), "fsdp")
    coupled = jnp.sum(coupled.astype(F32), axis=0).astype(BF16)
    coupled = lax.all_gather(spread(coupled, "section"), "fsdp", axis=0)
    far_near = lax.ppermute(
        jnp.stack(near[: count // 2 - 1]),
        "section",
        [(k + count // 2, k) for k in range(count // 2)],
    )

    micro_ids = jnp.arange(micro, dtype=jnp.int32)
    picked = plan[:, :, None] == micro_ids[None, None, :]
    cot_here = lax.dynamic_index_in_dim(reward_cot, fsdp_idx, 2, keepdims=False)
    pos_here = lax.dynamic_index_in_dim(reward_pos, fsdp_idx, 2, keepdims=False)
    cot_slot = jnp.sum(jnp.where(picked, cot_here[:, None, :], 0.0), axis=2)
    pos_slot = jnp.sum(jnp.where(picked, pos_here[:, None, :], 0), axis=2)
    row_ids = jnp.arange(row_count, dtype=jnp.int32)
    row_weight = jnp.where(pos_slot[:, :, None] == row_ids, cot_slot[:, :, None], 0.0)
    row_weight = row_weight.reshape(rows, 1)
    target = (jnp.arange(2, dtype=jnp.int32)[:, None] * micro + plan)[:, :, None] * row_count
    target = (target + row_ids).reshape(rows)
    place = (jnp.arange(rows, dtype=jnp.int32)[:, None] == target[None, :]).astype(BF16)
    top = top_grads.reshape(rows, width)
    head = reward_head.reshape(1, width)

    reached = top_products(top, row_weight, head, out_full, place, step)
    pre = exchanged(pre_parts(wide, in_t, far_in_t, step), "fsdp")
    pre = jnp.sum(pre.astype(F32), axis=0).astype(BF16)
    known = spread(jnp.concatenate([pre, reached], axis=0), "section")

    mirror_pre = lax.dynamic_index_in_dim(known, count - 1 - section_idx, 0, keepdims=False)
    own_pre = jnp.concatenate([pre[:half], mirror_pre[half:rows]], axis=0)
    firsts = exchanged(
        first_parts(top, row_weight, head, own_pre, place, blocks, step), "fsdp"
    )

    shared = exchanged(chain(section, known, coupled), "fsdp")
    own_in, far_in = input_grads(wide, shared, step)
    back_in = mirrored(far_in)
    cross = jnp.sum(shared[:, :units].astype(F32), axis=0).astype(BF16)
    cross = spread(cross, "fsdp")
    grad_out = output_grads(cross, firsts, near, far_near)
    grad_in = (own_in + back_in.astype(F32)).T
    return (grad_in[None], grad_out[None])


def solution(mesh):
    in_specs = (
        P("section", "fsdp", None),
        P("section", None, "fsdp"),
        P("section", None, "fsdp", None),
        P("section", None, "fsdp", None),
        P(None, None, "fsdp", None),
        P(),
        P(),
        P(),
        P(),
    )
    out_specs = (P("section", "fsdp", None), P("section", None, "fsdp"))
    return jax.shard_map(
        on_device, mesh=mesh, in_specs=in_specs, out_specs=out_specs, check_vma=False
    )
```

```python
import jax
import jax.numpy as jnp
from jax import lax
from jax.experimental import pallas as pl
from jax.experimental.pallas import tpu as pltpu
from jax.sharding import PartitionSpec as P


BF16 = jnp.bfloat16
F32 = jnp.float32
ROWS_OF_BOTH = (((0,), (0,)), ((), ()))
COLS_OF_BOTH = (((1,), (1,)), ((), ()))


def dot(left, right, dims=(((1,), (0,)), ((), ()))):
    return lax.dot_general(left, right, dims, preferred_element_type=F32)


def from_above(value, steps):
    count = lax.axis_size("section")
    return lax.ppermute(value, "section", [((k + steps) % count, k) for k in range(count)])


def mirrored(value):
    count = lax.axis_size("section")
    return lax.ppermute(value, "section", [(k, count - 1 - k) for k in range(count)])


def exchanged(parts, axis, groups=None):
    return lax.all_to_all(parts, axis, 0, 0, axis_index_groups=groups, tiled=True)


def crossed(value, mask):
    count = lax.axis_size("section")
    return lax.ppermute(value, "section", [(k, k ^ mask) for k in range(count)])


def same_core(count):
    return [list(range(core, count, 2)) for core in range(2)]


def from_other_core(value):
    count = lax.axis_size("fsdp")
    return lax.ppermute(value, "fsdp", [(f, f ^ 1) for f in range(count)])


def vmem():
    return pl.BlockSpec(memory_space=pltpu.VMEM)


def smem():
    return pl.BlockSpec(memory_space=pltpu.SMEM)


def couplings(section, in_t, out_t, near, count):
    units = in_t.shape[0]
    slots = len(near)

    def kernel(section_ref, in_ref, out_ref, *refs):
        dest, packed = refs[slots:]
        for slot in range(slots - 1):
            packed[slot] = refs[slot][...]
        for slot in range(slots):
            wrapped = section_ref[0] + slot + 1 >= count

            @pl.when(wrapped)
            def _():
                dest[slot] = dot(in_ref[...], refs[slot][...], COLS_OF_BOTH).astype(BF16)

            @pl.when(jnp.logical_not(wrapped))
            def _():
                dest[slot] = dot(refs[slot][...], out_ref[...], COLS_OF_BOTH).astype(BF16)

    return pl.pallas_call(
        kernel,
        out_shape=[
            jax.ShapeDtypeStruct((slots, units, units), BF16),
            jax.ShapeDtypeStruct((slots - 1,) + in_t.shape, BF16),
        ],
        in_specs=[smem()] + [vmem()] * (2 + slots),
        out_specs=[vmem(), vmem()],
        name="couplings",
    )(section, in_t, out_t, *near)


def laid_out(down, up, blocks, step):
    half, width = down.shape
    part = width // blocks

    def kernel(down_ref, up_ref, dest):
        for b in range(step):
            dest[b, :half] = down_ref[:, b * part : (b + 1) * part]
            dest[b, half:] = up_ref[:, b * part : (b + 1) * part]

    return pl.pallas_call(
        kernel,
        grid=(blocks // step,),
        out_shape=jax.ShapeDtypeStruct((blocks, 2 * half, part), BF16),
        in_specs=[pl.BlockSpec((half, step * part), lambda b: (0, b))] * 2,
        out_specs=pl.BlockSpec((step, 2 * half, part), lambda b: (b, 0, 0)),
        name="laid_out",
    )(down, up)


def stacked(pieces):
    count = len(pieces)
    length = pieces[0].shape[0]

    def kernel(*refs):
        for at in range(count):
            refs[count][at * length : (at + 1) * length] = refs[at][...]

    return pl.pallas_call(
        kernel,
        out_shape=jax.ShapeDtypeStruct((count * length,) + pieces[0].shape[1:], BF16),
        in_specs=[vmem()] * count,
        out_specs=vmem(),
        name="stacked",
    )(*pieces)


def folded(parts, copies, used):
    blocks, _, units = parts.shape

    def kernel(parts_ref, dest):
        total = parts_ref[0, :used].astype(F32)
        for b in range(1, blocks):
            total = total + parts_ref[b, :used].astype(F32)
        total = total.astype(BF16)
        for c in range(copies):
            dest[c] = total

    return pl.pallas_call(
        kernel,
        out_shape=jax.ShapeDtypeStruct((copies, used, units), BF16),
        in_specs=[vmem()],
        out_specs=vmem(),
        name="folded",
    )(parts)


def folded_with(parts, below, copies):
    blocks, rows, units = parts.shape

    def kernel(parts_ref, below_ref, dest, own):
        total = parts_ref[0].astype(F32)
        for b in range(1, blocks):
            total = total + parts_ref[b].astype(F32)
        total = total.astype(BF16)
        own[0] = total[: rows // 2]
        own[1] = total[rows // 2 :]
        for c in range(copies):
            dest[c, :rows] = total
            dest[c, rows:] = below_ref[...]

    return pl.pallas_call(
        kernel,
        out_shape=[
            jax.ShapeDtypeStruct((copies, 2 * rows, units), BF16),
            jax.ShapeDtypeStruct((2, rows // 2, units), BF16),
        ],
        in_specs=[vmem(), vmem()],
        out_specs=[vmem(), vmem()],
        name="folded_with",
    )(parts, below)


def pre_parts(wide, in_t, far_in_t, step):
    blocks, rows, part = wide.shape
    units = in_t.shape[0]
    half = rows // 2

    def kernel(wide_ref, in_ref, far_ref, dest):
        for b in range(step):
            dest[b, :half] = dot(wide_ref[b, :half], in_ref[...], COLS_OF_BOTH).astype(BF16)
            dest[b, half:] = dot(wide_ref[b, half:], far_ref[...], COLS_OF_BOTH).astype(BF16)

    return pl.pallas_call(
        kernel,
        grid=(blocks // step,),
        out_shape=jax.ShapeDtypeStruct((blocks, rows, units), BF16),
        in_specs=[
            pl.BlockSpec((step, rows, part), lambda b: (b, 0, 0)),
            pl.BlockSpec((units, part), lambda b: (0, 0)),
            pl.BlockSpec((units, part), lambda b: (0, 0)),
        ],
        out_specs=pl.BlockSpec((step, rows, units), lambda b: (b, 0, 0)),
        name="pre_parts",
    )(wide, in_t, far_in_t)


def top_products(top, row_weight, head, out_full, place, step):
    blocks, units, part = out_full.shape
    rows = top.shape[0]

    def kernel(top_ref, weight_ref, head_ref, out_ref, place_ref, dest, acc):
        at = pl.program_id(0)

        @pl.when(at == 0)
        def _():
            acc[...] = jnp.zeros_like(acc)

        first = (top_ref[...].astype(F32) + weight_ref[...] * head_ref[...]).astype(BF16)
        total = acc[...]
        for b in range(step):
            total = total + dot(first[:, b * part : (b + 1) * part], out_ref[b], COLS_OF_BOTH)
        acc[...] = total

        @pl.when(at == pl.num_programs(0) - 1)
        def _():
            dest[...] = dot(place_ref[...], acc[...].astype(BF16)).astype(BF16)

    return pl.pallas_call(
        kernel,
        grid=(blocks // step,),
        out_shape=jax.ShapeDtypeStruct((rows, units), BF16),
        in_specs=[
            pl.BlockSpec((rows, step * part), lambda b: (0, b)),
            pl.BlockSpec((rows, 1), lambda b: (0, 0)),
            pl.BlockSpec((1, step * part), lambda b: (0, b)),
            pl.BlockSpec((step, units, part), lambda b: (b, 0, 0)),
            pl.BlockSpec((rows, rows), lambda b: (0, 0)),
        ],
        out_specs=pl.BlockSpec((rows, units), lambda b: (0, 0)),
        scratch_shapes=[pltpu.VMEM((rows, units), F32)],
        name="top_products",
    )(top, row_weight, head, out_full, place)


def first_parts(top, row_weight, head, pre_down, pre_up, place, blocks, step):
    rows, width = top.shape
    half, units = pre_down.shape
    part = width // blocks

    def kernel(top_ref, weight_ref, head_ref, down_ref, up_ref, place_ref, dest):
        value = jnp.concatenate([down_ref[...], up_ref[...]], axis=0).astype(F32)
        hidden = (value * jax.nn.sigmoid(value)).astype(BF16)
        placed = dot(hidden, place_ref[...], ROWS_OF_BOTH).astype(BF16)
        first = (top_ref[...].astype(F32) + weight_ref[...] * head_ref[...]).astype(BF16)
        total = dot(placed, first).astype(BF16)
        for b in range(step):
            dest[b] = total[:, b * part : (b + 1) * part]

    return pl.pallas_call(
        kernel,
        grid=(blocks // step,),
        out_shape=jax.ShapeDtypeStruct((blocks, units, part), BF16),
        in_specs=[
            pl.BlockSpec((rows, step * part), lambda b: (0, b)),
            pl.BlockSpec((rows, 1), lambda b: (0, 0)),
            pl.BlockSpec((1, step * part), lambda b: (0, b)),
            pl.BlockSpec((half, units), lambda b: (0, 0)),
            pl.BlockSpec((half, units), lambda b: (0, 0)),
            pl.BlockSpec((rows, rows), lambda b: (0, 0)),
        ],
        out_specs=pl.BlockSpec((step, units, part), lambda b: (b, 0, 0)),
        name="first_parts",
    )(top, row_weight, head, pre_down, pre_up, place)


def chain(section, core, known, same, other):
    count, tall, units = known.shape
    rows = tall // 2
    half = rows // 2

    def kernel(section_ref, core_ref, known_ref, same_ref, other_ref, dest, reach, grads):
        even = core_ref[0] == 0
        own = section_ref[0]

        def pre_of(layer, other):
            return jnp.concatenate(
                [known_ref[layer, :half], known_ref[other, half:rows]], axis=0
            ).astype(F32)

        def coupling(upper, lower):
            gap = upper - lower
            if gap <= count // 2:
                at, slot = lower, gap - 1
            else:
                at, slot = upper, count - gap - 1
            place = jnp.bitwise_xor(own, at)
            mine, theirs = same_ref[slot, place], other_ref[slot, place]
            return jnp.concatenate(
                [jnp.where(even, mine, theirs), jnp.where(even, theirs, mine)], axis=0
            )

        for layer in range(count):
            reach[layer] = known_ref[layer, rows:].astype(F32)
        for layer in range(count - 1, -1, -1):
            pre = pre_of(layer, count - 1 - layer)
            sig = jax.nn.sigmoid(pre)
            grad_pre = (reach[layer] * sig * (1.0 + pre * (1.0 - sig))).astype(BF16)
            grads[layer] = grad_pre
            if layer > 0:
                lower = jnp.concatenate([coupling(layer, low) for low in range(layer)], axis=1)
                update = dot(grad_pre, lower)
                for low in range(layer):
                    reach[low] += update[:, low * units : (low + 1) * units]
        far = count - 1 - own
        pre = pre_of(own, far)
        hidden = (pre * jax.nn.sigmoid(pre)).astype(BF16)
        above = jnp.concatenate(
            [grads[jnp.minimum(own + up, count - 1)] for up in range(1, count)], axis=1
        )
        cross = dot(hidden, above, ROWS_OF_BOTH)
        sent = jnp.concatenate([grads[own][:half], grads[far][half:]], axis=0)
        for up in range(count):
            if up == 0:
                dest[up, :units] = jnp.zeros((units, units), BF16)
            else:
                block = cross[:, (up - 1) * units : up * units]
                dest[up, :units] = jnp.where(own + up < count, block, 0.0).astype(BF16)
            dest[up, units:] = sent

    return pl.pallas_call(
        kernel,
        out_shape=jax.ShapeDtypeStruct((count, units + rows, units), BF16),
        in_specs=[smem(), smem(), vmem(), vmem(), vmem()],
        out_specs=vmem(),
        scratch_shapes=[
            pltpu.VMEM((count, rows, units), F32),
            pltpu.VMEM((count, rows, units), BF16),
        ],
        name="chain",
    )(section, core, known, same, other)


def input_grads(wide, shared, step):
    blocks, rows, part = wide.shape
    tall, units = shared.shape[1:]
    half = rows // 2
    skip = tall - rows

    def kernel(wide_ref, shared_ref, own, far, own_acc, far_acc):
        at = pl.program_id(0)

        @pl.when(at == 0)
        def _():
            own_acc[...] = jnp.zeros_like(own_acc)
            far_acc[...] = jnp.zeros_like(far_acc)

        for b in range(step):
            own_acc[...] += dot(
                shared_ref[b, skip : skip + half], wide_ref[b, :half], ROWS_OF_BOTH
            )
            far_acc[...] += dot(shared_ref[b, skip + half :], wide_ref[b, half:], ROWS_OF_BOTH)

        @pl.when(at == pl.num_programs(0) - 1)
        def _():
            own[...] = own_acc[...]
            far[...] = far_acc[...].astype(BF16)

    return pl.pallas_call(
        kernel,
        grid=(blocks // step,),
        out_shape=[
            jax.ShapeDtypeStruct((units, part), F32),
            jax.ShapeDtypeStruct((units, part), BF16),
        ],
        in_specs=[
            pl.BlockSpec((step, rows, part), lambda b: (b, 0, 0)),
            pl.BlockSpec((step, tall, units), lambda b: (b, 0, 0)),
        ],
        out_specs=[
            pl.BlockSpec((units, part), lambda b: (0, 0)),
            pl.BlockSpec((units, part), lambda b: (0, 0)),
        ],
        scratch_shapes=[pltpu.VMEM((units, part), F32), pltpu.VMEM((units, part), F32)],
        name="input_grads",
    )(wide, shared)


def output_grads(cross, firsts, near, far):
    count, units, _ = cross.shape
    blocks, _, part = firsts.shape
    slots = len(near)

    def kernel(cross_ref, first_ref, far_ref, *refs):
        dest = refs[slots]
        total = jnp.zeros((units, part), F32)
        for b in range(blocks):
            total = total + first_ref[b].astype(F32)
        for up in range(1, count):
            other = refs[up - 1][...] if up <= slots else far_ref[up - 1 - slots]
            total = total + dot(cross_ref[up], other)
        dest[...] = total

    return pl.pallas_call(
        kernel,
        out_shape=jax.ShapeDtypeStruct((units, part), F32),
        in_specs=[vmem()] * (3 + slots),
        out_specs=vmem(),
        name="output_grads",
    )(cross, firsts, far, *near)


def on_device(
    branch_in,
    branch_out,
    down_inputs,
    up_inputs,
    top_grads,
    plan,
    reward_pos,
    reward_cot,
    reward_head,
):
    count = lax.axis_size("section")
    blocks = lax.axis_size("fsdp")
    section_idx = lax.axis_index("section")
    fsdp_idx = lax.axis_index("fsdp")
    section = section_idx.astype(jnp.int32).reshape(1)
    _, micro, row_count, width = down_inputs.shape
    units = branch_in.shape[2]
    half = micro * row_count
    rows = 2 * half
    step = 4

    core = (fsdp_idx % 2).astype(jnp.int32).reshape(1)
    groups = same_core(blocks)

    in_t = branch_in[0].T
    out_t = branch_out[0]
    down = down_inputs[0].reshape(half, width)
    up = up_inputs[0].reshape(half, width)
    out_full = lax.all_gather(out_t, "fsdp", axis=0)
    wide = exchanged(laid_out(down, up, blocks, step), "fsdp")
    near = []
    for above in range(1, count // 2 + 1):
        near.append(from_above(jnp.where(section_idx >= above, in_t, out_t), above))
    far_in_t = mirrored(in_t)

    coupled, packed = couplings(section, in_t, out_t, near, count)
    coupled = exchanged(coupled.reshape(blocks, -1, units), "fsdp")
    coupled = folded(coupled, 1, coupled.shape[1])
    for unit in (1, 4):
        coupled = stacked(
            [coupled] + [crossed(coupled, unit * times) for times in range(1, 4)]
        )
    coupled_same = lax.all_gather(coupled, "fsdp", axis=0, axis_index_groups=groups)
    coupled_other = from_other_core(coupled_same)
    far_near = lax.ppermute(
        packed, "section", [(k + count // 2, k) for k in range(count // 2)]
    )

    micro_ids = jnp.arange(micro, dtype=jnp.int32)
    picked = plan[:, :, None] == micro_ids[None, None, :]
    cot_here = lax.dynamic_index_in_dim(reward_cot, fsdp_idx, 2, keepdims=False)
    pos_here = lax.dynamic_index_in_dim(reward_pos, fsdp_idx, 2, keepdims=False)
    cot_slot = jnp.sum(jnp.where(picked, cot_here[:, None, :], 0.0), axis=2)
    pos_slot = jnp.sum(jnp.where(picked, pos_here[:, None, :], 0), axis=2)
    row_ids = jnp.arange(row_count, dtype=jnp.int32)
    row_weight = jnp.where(pos_slot[:, :, None] == row_ids, cot_slot[:, :, None], 0.0)
    row_weight = row_weight.reshape(rows, 1)
    target = (jnp.arange(2, dtype=jnp.int32)[:, None] * micro + plan)[:, :, None] * row_count
    target = (target + row_ids).reshape(rows)
    place = (jnp.arange(rows, dtype=jnp.int32)[:, None] == target[None, :]).astype(BF16)
    top = top_grads.reshape(rows, width)
    head = reward_head.reshape(1, width)

    reached = top_products(top, row_weight, head, out_full, place, step)
    parts = pre_parts(wide, in_t, far_in_t, step)
    parts = exchanged(parts, "fsdp")
    known, own_pre = folded_with(parts, reached, count)
    mirror_pre = mirrored(own_pre[1])
    known = exchanged(known, "section")
    firsts = first_parts(top, row_weight, head, own_pre[0], mirror_pre, place, blocks, step)
    firsts = exchanged(firsts, "fsdp")

    shared = chain(section, core, known, coupled_same, coupled_other)
    shared = exchanged(shared, "fsdp")
    own_in, far_in = input_grads(wide, shared, step)
    back_in = mirrored(far_in)
    cross = exchanged(folded(shared, blocks, units), "fsdp")
    grad_out = output_grads(cross, firsts, near, far_near)
    grad_in = (own_in + back_in.astype(F32)).T
    return (grad_in[None], grad_out[None])


def solution(mesh):
    in_specs = (
        P("section", "fsdp", None),
        P("section", None, "fsdp"),
        P("section", None, "fsdp", None),
        P("section", None, "fsdp", None),
        P(None, None, "fsdp", None),
        P(),
        P(),
        P(),
        P(),
    )
    out_specs = (P("section", "fsdp", None), P("section", None, "fsdp"))
    return jax.shard_map(
        on_device, mesh=mesh, in_specs=in_specs, out_specs=out_specs, check_vma=False
    )
```

```python
import jax
import jax.numpy as jnp
from jax import lax
from jax.experimental import pallas as pl
from jax.experimental.pallas import tpu as pltpu
from jax.sharding import PartitionSpec as P


BF16 = jnp.bfloat16
F32 = jnp.float32
ROWS_OF_BOTH = (((0,), (0,)), ((), ()))
COLS_OF_BOTH = (((1,), (1,)), ((), ()))


def dot(left, right, dims=(((1,), (0,)), ((), ()))):
    return lax.dot_general(left, right, dims, preferred_element_type=F32)


def from_above(value, steps):
    count = lax.axis_size("section")
    return lax.ppermute(value, "section", [((k + steps) % count, k) for k in range(count)])


def mirrored(value):
    count = lax.axis_size("section")
    return lax.ppermute(value, "section", [(k, count - 1 - k) for k in range(count)])


def exchanged(parts, axis, groups=None):
    return lax.all_to_all(parts, axis, 0, 0, axis_index_groups=groups, tiled=True)


def same_core(count):
    return [list(range(core, count, 2)) for core in range(2)]


def from_other_core(value):
    count = lax.axis_size("fsdp")
    return lax.ppermute(value, "fsdp", [(f, f ^ 1) for f in range(count)])


def vmem():
    return pl.BlockSpec(memory_space=pltpu.VMEM)


def smem():
    return pl.BlockSpec(memory_space=pltpu.SMEM)


def couplings(section, in_t, out_t, near, count):
    units = in_t.shape[0]
    slots = len(near)

    def kernel(section_ref, in_ref, out_ref, *refs):
        dest = refs[slots]
        for slot in range(slots):
            wrapped = section_ref[0] + slot + 1 >= count

            @pl.when(wrapped)
            def _():
                dest[slot] = dot(in_ref[...], refs[slot][...], COLS_OF_BOTH).astype(BF16)

            @pl.when(jnp.logical_not(wrapped))
            def _():
                dest[slot] = dot(refs[slot][...], out_ref[...], COLS_OF_BOTH).astype(BF16)

    return pl.pallas_call(
        kernel,
        out_shape=jax.ShapeDtypeStruct((slots, units, units), BF16),
        in_specs=[smem()] + [vmem()] * (2 + slots),
        out_specs=vmem(),
        name="couplings",
    )(section, in_t, out_t, *near)


def laid_out(down, up, blocks, step):
    half, width = down.shape
    part = width // blocks

    def kernel(down_ref, up_ref, dest):
        for b in range(step):
            dest[b, :half] = down_ref[:, b * part : (b + 1) * part]
            dest[b, half:] = up_ref[:, b * part : (b + 1) * part]

    return pl.pallas_call(
        kernel,
        grid=(blocks // step,),
        out_shape=jax.ShapeDtypeStruct((blocks, 2 * half, part), BF16),
        in_specs=[pl.BlockSpec((half, step * part), lambda b: (0, b))] * 2,
        out_specs=pl.BlockSpec((step, 2 * half, part), lambda b: (b, 0, 0)),
        name="laid_out",
    )(down, up)


def folded(parts, copies, used):
    blocks, _, units = parts.shape

    def kernel(parts_ref, dest):
        total = parts_ref[0, :used].astype(F32)
        for b in range(1, blocks):
            total = total + parts_ref[b, :used].astype(F32)
        total = total.astype(BF16)
        for c in range(copies):
            dest[c] = total

    return pl.pallas_call(
        kernel,
        out_shape=jax.ShapeDtypeStruct((copies, used, units), BF16),
        in_specs=[vmem()],
        out_specs=vmem(),
        name="folded",
    )(parts)


def folded_with(parts, below, copies, lead):
    blocks, rows, units = parts.shape
    half = (rows - lead) // 2

    def kernel(parts_ref, below_ref, dest, own):
        total = parts_ref[0].astype(F32)
        for b in range(1, blocks):
            total = total + parts_ref[b].astype(F32)
        total = total.astype(BF16)
        own[0] = total[lead : lead + half]
        own[1] = total[lead + half :]
        for c in range(copies):
            dest[c, :rows] = total
            dest[c, rows:] = below_ref[...]

    return pl.pallas_call(
        kernel,
        out_shape=[
            jax.ShapeDtypeStruct((copies, rows + below.shape[0], units), BF16),
            jax.ShapeDtypeStruct((2, half, units), BF16),
        ],
        in_specs=[vmem(), vmem()],
        out_specs=[vmem(), vmem()],
        name="folded_with",
    )(parts, below)


def row_setup(fsdp, plan, reward_pos, reward_cot, row_count):
    directions, micro = plan.shape
    rows = directions * micro * row_count

    def kernel(fsdp_ref, plan_ref, pos_ref, cot_ref, weight, place):
        at = fsdp_ref[0]
        row = lax.broadcasted_iota(jnp.int32, (row_count, 128), 0)
        wide_row = lax.broadcasted_iota(jnp.int32, (row_count, rows), 0)
        wide_col = lax.broadcasted_iota(jnp.int32, (row_count, rows), 1)
        for d in range(directions):
            for j in range(micro):
                ident = plan_ref[d, j]
                base = (d * micro + j) * row_count
                spot = (d * micro + ident) * row_count
                value = jnp.where(row == pos_ref[d, ident, at], cot_ref[d, ident, at], 0.0)
                weight[base : base + row_count] = value
                place[base : base + row_count] = jnp.where(
                    wide_col == wide_row + spot, 1.0, 0.0
                )

    return pl.pallas_call(
        kernel,
        out_shape=[
            jax.ShapeDtypeStruct((rows, 128), F32),
            jax.ShapeDtypeStruct((rows, rows), F32),
        ],
        in_specs=[smem()] * 4,
        out_specs=[vmem(), vmem()],
        name="row_setup",
    )(fsdp, plan, reward_pos, reward_cot)


def pre_parts(wide, coupled, in_t, far_in_t, step):
    blocks, rows, part = wide.shape
    units = in_t.shape[0]
    lead = coupled.shape[1]
    half = rows // 2

    def kernel(wide_ref, coupled_ref, in_ref, far_ref, dest):
        for b in range(step):
            dest[b, :lead] = coupled_ref[b]
            dest[b, lead : lead + half] = dot(
                wide_ref[b, :half], in_ref[...], COLS_OF_BOTH
            ).astype(BF16)
            dest[b, lead + half :] = dot(
                wide_ref[b, half:], far_ref[...], COLS_OF_BOTH
            ).astype(BF16)

    return pl.pallas_call(
        kernel,
        grid=(blocks // step,),
        out_shape=jax.ShapeDtypeStruct((blocks, lead + rows, units), BF16),
        in_specs=[
            pl.BlockSpec((step, rows, part), lambda b: (b, 0, 0)),
            pl.BlockSpec((step, lead, units), lambda b: (b, 0, 0)),
            pl.BlockSpec((units, part), lambda b: (0, 0)),
            pl.BlockSpec((units, part), lambda b: (0, 0)),
        ],
        out_specs=pl.BlockSpec((step, lead + rows, units), lambda b: (b, 0, 0)),
        name="pre_parts",
    )(wide, coupled, in_t, far_in_t)


def top_products(top, row_weight, head, out_full, place, step):
    blocks, units, part = out_full.shape
    rows = top.shape[0]

    def kernel(top_ref, weight_ref, head_ref, out_ref, place_ref, dest, acc):
        at = pl.program_id(0)

        @pl.when(at == 0)
        def _():
            acc[...] = jnp.zeros_like(acc)

        first = top_ref[...].astype(F32) + weight_ref[:, :1] * head_ref[...]
        first = first.astype(BF16)
        total = acc[...]
        for b in range(step):
            total = total + dot(first[:, b * part : (b + 1) * part], out_ref[b], COLS_OF_BOTH)
        acc[...] = total

        @pl.when(at == pl.num_programs(0) - 1)
        def _():
            dest[...] = dot(
                place_ref[...].astype(BF16), acc[...].astype(BF16), ROWS_OF_BOTH
            ).astype(BF16)

    return pl.pallas_call(
        kernel,
        grid=(blocks // step,),
        out_shape=jax.ShapeDtypeStruct((rows, units), BF16),
        in_specs=[
            pl.BlockSpec((rows, step * part), lambda b: (0, b)),
            pl.BlockSpec((rows, 128), lambda b: (0, 0)),
            pl.BlockSpec((1, step * part), lambda b: (0, b)),
            pl.BlockSpec((step, units, part), lambda b: (b, 0, 0)),
            pl.BlockSpec((rows, rows), lambda b: (0, 0)),
        ],
        out_specs=pl.BlockSpec((rows, units), lambda b: (0, 0)),
        scratch_shapes=[pltpu.VMEM((rows, units), F32)],
        name="top_products",
    )(top, row_weight, head, out_full, place)


def first_parts(top, row_weight, head, pre_down, pre_up, place, blocks, step):
    rows, width = top.shape
    half, units = pre_down.shape
    part = width // blocks

    def kernel(top_ref, weight_ref, head_ref, down_ref, up_ref, place_ref, dest):
        value = jnp.concatenate([down_ref[...], up_ref[...]], axis=0).astype(F32)
        hidden = (value * jax.nn.sigmoid(value)).astype(BF16)
        placed = dot(place_ref[...].astype(BF16), hidden).astype(BF16)
        first = top_ref[...].astype(F32) + weight_ref[:, :1] * head_ref[...]
        first = first.astype(BF16)
        total = dot(placed, first, ROWS_OF_BOTH).astype(BF16)
        for b in range(step):
            dest[b] = total[:, b * part : (b + 1) * part]

    return pl.pallas_call(
        kernel,
        grid=(blocks // step,),
        out_shape=jax.ShapeDtypeStruct((blocks, units, part), BF16),
        in_specs=[
            pl.BlockSpec((rows, step * part), lambda b: (0, b)),
            pl.BlockSpec((rows, 128), lambda b: (0, 0)),
            pl.BlockSpec((1, step * part), lambda b: (0, b)),
            pl.BlockSpec((half, units), lambda b: (0, 0)),
            pl.BlockSpec((half, units), lambda b: (0, 0)),
            pl.BlockSpec((rows, rows), lambda b: (0, 0)),
        ],
        out_specs=pl.BlockSpec((step, units, part), lambda b: (b, 0, 0)),
        name="first_parts",
    )(top, row_weight, head, pre_down, pre_up, place)


def chain(section, core, known, same, other):
    count, tall, units = known.shape
    lead = same.shape[2]
    rows = (tall - lead) // 2
    half = rows // 2

    def kernel(section_ref, core_ref, known_ref, same_ref, other_ref, dest, reach, grads):
        even = core_ref[0] == 0
        own = section_ref[0]

        def pre_of(layer, other):
            return jnp.concatenate(
                [
                    known_ref[layer, lead : lead + half],
                    known_ref[other, lead + half : lead + rows],
                ],
                axis=0,
            ).astype(F32)

        def coupling(upper, lower):
            gap = upper - lower
            if gap <= count // 2:
                at, slot = lower, gap - 1
            else:
                at, slot = upper, count - gap - 1
            mine, theirs = same_ref[slot, at], other_ref[slot, at]
            return jnp.concatenate(
                [jnp.where(even, mine, theirs), jnp.where(even, theirs, mine)], axis=0
            )

        for layer in range(count):
            reach[layer] = known_ref[layer, lead + rows :].astype(F32)
        for layer in range(count - 1, -1, -1):
            pre = pre_of(layer, count - 1 - layer)
            sig = jax.nn.sigmoid(pre)
            grad_pre = (reach[layer] * sig * (1.0 + pre * (1.0 - sig))).astype(BF16)
            grads[layer] = grad_pre
            if layer > 0:
                lower = jnp.concatenate([coupling(layer, low) for low in range(layer)], axis=1)
                update = dot(grad_pre, lower)
                for low in range(layer):
                    reach[low] += update[:, low * units : (low + 1) * units]
        far = count - 1 - own
        pre = pre_of(own, far)
        hidden = (pre * jax.nn.sigmoid(pre)).astype(BF16)
        above = jnp.concatenate(
            [grads[jnp.minimum(own + up, count - 1)] for up in range(1, count)], axis=1
        )
        cross = dot(hidden, above, ROWS_OF_BOTH)
        sent = jnp.concatenate([grads[own][:half], grads[far][half:]], axis=0)
        for up in range(count):
            if up == 0:
                dest[up, :units] = jnp.zeros((units, units), BF16)
            else:
                block = cross[:, (up - 1) * units : up * units]
                dest[up, :units] = jnp.where(own + up < count, block, 0.0).astype(BF16)
            dest[up, units:] = sent

    return pl.pallas_call(
        kernel,
        out_shape=jax.ShapeDtypeStruct((count, units + rows, units), BF16),
        in_specs=[smem(), smem(), vmem(), vmem(), vmem()],
        out_specs=vmem(),
        scratch_shapes=[
            pltpu.VMEM((count, rows, units), F32),
            pltpu.VMEM((count, rows, units), BF16),
        ],
        name="chain",
    )(section, core, known, same, other)


def input_grads(wide, shared, step, side, kind):
    blocks, rows, part = wide.shape
    tall, units = shared.shape[1:]
    half = rows // 2
    skip = tall - rows + side * half

    def kernel(wide_ref, shared_ref, dest, acc):
        at = pl.program_id(0)

        @pl.when(at == 0)
        def _():
            acc[...] = jnp.zeros_like(acc)

        total = acc[...]
        for b in range(step):
            total = total + dot(shared_ref[b, skip : skip + half], wide_ref[b], ROWS_OF_BOTH)
        acc[...] = total

        @pl.when(at == pl.num_programs(0) - 1)
        def _():
            dest[...] = acc[...].astype(kind)

    return pl.pallas_call(
        kernel,
        grid=(blocks // step,),
        out_shape=jax.ShapeDtypeStruct((units, part), kind),
        in_specs=[
            pl.BlockSpec((step, half, part), lambda b: (b, side, 0)),
            pl.BlockSpec((step, tall, units), lambda b: (b, 0, 0)),
        ],
        out_specs=pl.BlockSpec((units, part), lambda b: (0, 0)),
        scratch_shapes=[pltpu.VMEM((units, part), F32)],
    )(wide, shared)


def output_grads(section, cross, first, near, far):
    count, units, _ = cross.shape
    part = first.shape[1]
    slots = len(near)
    upper = count // 2

    def kernel(section_ref, cross_ref, first_ref, far_ref, *refs):
        dest = refs[slots]
        own = section_ref[0]
        total = first_ref[...].astype(F32)
        for up in range(1, slots + 1):
            total = total + dot(cross_ref[up], refs[up - 1][...])
        dest[...] = total
        for at in range(1, count - upper):

            @pl.when(at > own)
            def _():
                dest[...] += dot(cross_ref[at + upper - own], far_ref[at])

    return pl.pallas_call(
        kernel,
        out_shape=jax.ShapeDtypeStruct((units, part), F32),
        in_specs=[smem()] + [vmem()] * (3 + slots),
        out_specs=vmem(),
        name="output_grads",
    )(section, cross, first, far, *near)


def on_device(
    branch_in,
    branch_out,
    down_inputs,
    up_inputs,
    top_grads,
    plan,
    reward_pos,
    reward_cot,
    reward_head,
):
    count = lax.axis_size("section")
    blocks = lax.axis_size("fsdp")
    section_idx = lax.axis_index("section")
    fsdp_idx = lax.axis_index("fsdp")
    section = section_idx.astype(jnp.int32).reshape(1)
    _, micro, row_count, width = down_inputs.shape
    units = branch_in.shape[2]
    part = width // blocks
    half = micro * row_count
    rows = 2 * half
    step = 4

    core = (fsdp_idx % 2).astype(jnp.int32).reshape(1)
    groups = same_core(blocks)

    in_t = branch_in[0].T
    out_t = branch_out[0]
    down = down_inputs[0].reshape(half, width)
    up = up_inputs[0].reshape(half, width)
    out_full = lax.all_gather(out_t, "fsdp", axis=0)
    wide = exchanged(laid_out(down, up, blocks, step), "fsdp")
    near = []
    for above in range(1, count // 2 + 1):
        near.append(from_above(jnp.where(section_idx >= above, in_t, out_t), above))
    far_in_t = mirrored(in_t)

    partner = lax.ppermute(
        in_t, "section", [(k + count // 2, k) for k in range(count // 2)]
    )
    far_all = lax.all_gather(
        partner,
        "section",
        axis=0,
        axis_index_groups=[list(range(count // 2)), list(range(count // 2, count))],
    )

    coupled = couplings(section, in_t, out_t, near, count).reshape(blocks, -1, units)
    lead = coupled.shape[1]
    row_weight, place = row_setup(
        fsdp_idx.astype(jnp.int32).reshape(1), plan, reward_pos, reward_cot, row_count
    )
    top = top_grads.reshape(rows, width)
    head = reward_head.reshape(1, width)
    parts = pre_parts(wide, coupled, in_t, far_in_t, step)
    parts = exchanged(parts, "fsdp")
    reached = top_products(top, row_weight, head, out_full, place, step)
    known, own_pre = folded_with(parts, reached, count, lead)
    mirror_pre = mirrored(own_pre[1])
    known = exchanged(known, "section")
    firsts = first_parts(top, row_weight, head, own_pre[0], mirror_pre, place, blocks, step)
    first = lax.psum_scatter(
        firsts.reshape(blocks * units, part), "fsdp", scatter_dimension=0, tiled=True
    )
    coupled = known[:, :lead]
    coupled_same = exchanged(
        jnp.broadcast_to(coupled[None], (blocks // 2,) + coupled.shape), "fsdp", groups
    )
    coupled_other = from_other_core(coupled_same)

    shared = chain(section, core, known, coupled_same, coupled_other)
    shared = exchanged(shared, "fsdp")
    far_in = input_grads(wide, shared, step, 1, BF16)
    back_in = mirrored(far_in)
    cross = exchanged(folded(shared, blocks, units), "fsdp")
    own_in = input_grads(wide, shared, step, 0, F32)
    grad_out = output_grads(section, cross, first, near, far_all)
    grad_in = (own_in + back_in.astype(F32)).T
    return (grad_in[None], grad_out[None])


def solution(mesh):
    in_specs = (
        P("section", "fsdp", None),
        P("section", None, "fsdp"),
        P("section", None, "fsdp", None),
        P("section", None, "fsdp", None),
        P(None, None, "fsdp", None),
        P(),
        P(),
        P(),
        P(),
    )
    out_specs = (P("section", "fsdp", None), P("section", None, "fsdp"))
    return jax.shard_map(
        on_device, mesh=mesh, in_specs=in_specs, out_specs=out_specs, check_vma=False
    )
```

```python
import jax
import jax.numpy as jnp
from jax import lax
from jax.experimental import pallas as pl
from jax.experimental.pallas import tpu as pltpu
from jax.sharding import PartitionSpec as P


BF16 = jnp.bfloat16
F32 = jnp.float32
ROWS_OF_BOTH = (((0,), (0,)), ((), ()))
COLS_OF_BOTH = (((1,), (1,)), ((), ()))


def dot(left, right, dims=(((1,), (0,)), ((), ()))):
    return lax.dot_general(left, right, dims, preferred_element_type=F32)


LOWER_OFFSETS = (0, -3, -1, 4)
UPPER_OFFSETS = (1, 2, 3, -2)


def inside_half(value, steps, ends):
    ring = lax.axis_size("section") // 2
    pairs = []
    for base in (0, ring):
        pairs += [(base + (z + steps) % ring, base + z) for z in range(ends)]
    return lax.ppermute(value, "section", pairs)


def across(value, slot):
    ring = lax.axis_size("section") // 2
    low, high = LOWER_OFFSETS[slot], UPPER_OFFSETS[slot]
    pairs = [(ring + (z - high) % ring, ring + z) for z in range(ring)]
    if low:
        pairs += [((z + low) % ring, z) for z in range(ring)]
    return lax.ppermute(value, "section", pairs)


def mirrored(value):
    count = lax.axis_size("section")
    return lax.ppermute(value, "section", [(k, count - 1 - k) for k in range(count)])


def exchanged(parts, axis, groups=None):
    return lax.all_to_all(parts, axis, 0, 0, axis_index_groups=groups, tiled=True)


def same_core(count):
    return [list(range(core, count, 2)) for core in range(2)]


def from_other_core(value):
    count = lax.axis_size("fsdp")
    return lax.ppermute(value, "fsdp", [(f, f ^ 1) for f in range(count)])


def vmem():
    return pl.BlockSpec(memory_space=pltpu.VMEM)


def smem():
    return pl.BlockSpec(memory_space=pltpu.SMEM)


def couplings(section, in_t, out_t, partner, inner, outer, count):
    units = in_t.shape[0]
    ring = count // 2
    slots = len(inner)

    def kernel(section_ref, in_ref, out_ref, partner_ref, *refs):
        dest = refs[2 * slots]
        own = section_ref[0]
        upper = own >= ring

        def store(slot, other, as_lower):
            @pl.when(as_lower)
            def _():
                dest[slot] = dot(other[...], out_ref[...], COLS_OF_BOTH).astype(BF16)

            @pl.when(jnp.logical_not(as_lower))
            def _():
                dest[slot] = dot(in_ref[...], other[...], COLS_OF_BOTH).astype(BF16)

        for slot in range(slots):
            store(slot, refs[slot], jnp.where(upper, own - ring, own) + slot + 1 < ring)
        for slot in range(slots):
            other = refs[slots + slot]
            if LOWER_OFFSETS[slot] == 0:

                @pl.when(upper)
                def _():
                    dest[slots + slot] = dot(in_ref[...], other[...], COLS_OF_BOTH).astype(BF16)

                @pl.when(jnp.logical_not(upper))
                def _():
                    value = dot(partner_ref[...], out_ref[...], COLS_OF_BOTH)
                    dest[slots + slot] = value.astype(BF16)
            else:
                store(slots + slot, other, jnp.logical_not(upper))

    return pl.pallas_call(
        kernel,
        out_shape=jax.ShapeDtypeStruct((2 * slots, units, units), BF16),
        in_specs=[smem()] + [vmem()] * (3 + 2 * slots),
        out_specs=vmem(),
        name="couplings",
    )(section, in_t, out_t, partner, *inner, *outer)


def laid_out(down, up, blocks, step):
    half, width = down.shape
    part = width // blocks

    def kernel(down_ref, up_ref, dest):
        for b in range(step):
            dest[b, :half] = down_ref[:, b * part : (b + 1) * part]
            dest[b, half:] = up_ref[:, b * part : (b + 1) * part]

    return pl.pallas_call(
        kernel,
        grid=(blocks // step,),
        out_shape=jax.ShapeDtypeStruct((blocks, 2 * half, part), BF16),
        in_specs=[pl.BlockSpec((half, step * part), lambda b: (0, b))] * 2,
        out_specs=pl.BlockSpec((step, 2 * half, part), lambda b: (b, 0, 0)),
        name="laid_out",
    )(down, up)


def folded(parts, copies, used):
    blocks, _, units = parts.shape

    def kernel(parts_ref, dest):
        total = parts_ref[0, :used].astype(F32)
        for b in range(1, blocks):
            total = total + parts_ref[b, :used].astype(F32)
        total = total.astype(BF16)
        for c in range(copies):
            dest[c] = total

    return pl.pallas_call(
        kernel,
        out_shape=jax.ShapeDtypeStruct((copies, used, units), BF16),
        in_specs=[vmem()],
        out_specs=vmem(),
        name="folded",
    )(parts)


def folded_with(parts, below, copies, lead):
    blocks, rows, units = parts.shape
    half = (rows - lead) // 2

    def kernel(parts_ref, below_ref, dest, own):
        total = parts_ref[0].astype(F32)
        for b in range(1, blocks):
            total = total + parts_ref[b].astype(F32)
        total = total.astype(BF16)
        own[...] = total[lead : lead + half]
        for c in range(copies):
            dest[c, :rows] = total
            dest[c, rows:] = below_ref[...]

    return pl.pallas_call(
        kernel,
        out_shape=[
            jax.ShapeDtypeStruct((copies, rows + below.shape[0], units), BF16),
            jax.ShapeDtypeStruct((half, units), BF16),
        ],
        in_specs=[vmem(), vmem()],
        out_specs=[vmem(), vmem()],
        name="folded_with",
    )(parts, below)


def row_setup(fsdp, plan, reward_pos, reward_cot, row_count):
    directions, micro = plan.shape
    rows = directions * micro * row_count

    def kernel(fsdp_ref, plan_ref, pos_ref, cot_ref, weight, place):
        at = fsdp_ref[0]
        row = lax.broadcasted_iota(jnp.int32, (row_count, 128), 0)
        wide_row = lax.broadcasted_iota(jnp.int32, (row_count, rows), 0)
        wide_col = lax.broadcasted_iota(jnp.int32, (row_count, rows), 1)
        for d in range(directions):
            for j in range(micro):
                ident = plan_ref[d, j]
                base = (d * micro + j) * row_count
                spot = (d * micro + ident) * row_count
                value = jnp.where(row == pos_ref[d, ident, at], cot_ref[d, ident, at], 0.0)
                weight[base : base + row_count] = value
                place[base : base + row_count] = jnp.where(
                    wide_col == wide_row + spot, 1.0, 0.0
                )

    return pl.pallas_call(
        kernel,
        out_shape=[
            jax.ShapeDtypeStruct((rows, 128), F32),
            jax.ShapeDtypeStruct((rows, rows), F32),
        ],
        in_specs=[smem()] * 4,
        out_specs=[vmem(), vmem()],
        name="row_setup",
    )(fsdp, plan, reward_pos, reward_cot)


def pre_parts(wide, coupled, in_t, far_in_t, step):
    blocks, rows, part = wide.shape
    units = in_t.shape[0]
    lead = coupled.shape[1]
    half = rows // 2

    def kernel(wide_ref, coupled_ref, in_ref, far_ref, dest):
        for b in range(step):
            dest[b, :lead] = coupled_ref[b]
            dest[b, lead : lead + half] = dot(
                wide_ref[b, :half], in_ref[...], COLS_OF_BOTH
            ).astype(BF16)
            dest[b, lead + half :] = dot(
                wide_ref[b, half:], far_ref[...], COLS_OF_BOTH
            ).astype(BF16)

    return pl.pallas_call(
        kernel,
        grid=(blocks // step,),
        out_shape=jax.ShapeDtypeStruct((blocks, lead + rows, units), BF16),
        in_specs=[
            pl.BlockSpec((step, rows, part), lambda b: (b, 0, 0)),
            pl.BlockSpec((step, lead, units), lambda b: (b, 0, 0)),
            pl.BlockSpec((units, part), lambda b: (0, 0)),
            pl.BlockSpec((units, part), lambda b: (0, 0)),
        ],
        out_specs=pl.BlockSpec((step, lead + rows, units), lambda b: (b, 0, 0)),
        name="pre_parts",
    )(wide, coupled, in_t, far_in_t)


def top_products(top, row_weight, head, out_full, place, step):
    blocks, units, part = out_full.shape
    rows = top.shape[0]

    def kernel(top_ref, weight_ref, head_ref, out_ref, place_ref, dest, acc):
        at = pl.program_id(0)

        @pl.when(at == 0)
        def _():
            acc[...] = jnp.zeros_like(acc)

        first = top_ref[...].astype(F32) + weight_ref[:, :1] * head_ref[...]
        first = first.astype(BF16)
        total = acc[...]
        for b in range(step):
            total = total + dot(first[:, b * part : (b + 1) * part], out_ref[b], COLS_OF_BOTH)
        acc[...] = total

        @pl.when(at == pl.num_programs(0) - 1)
        def _():
            dest[...] = dot(
                place_ref[...].astype(BF16), acc[...].astype(BF16), ROWS_OF_BOTH
            ).astype(BF16)

    return pl.pallas_call(
        kernel,
        grid=(blocks // step,),
        out_shape=jax.ShapeDtypeStruct((rows, units), BF16),
        in_specs=[
            pl.BlockSpec((rows, step * part), lambda b: (0, b)),
            pl.BlockSpec((rows, 128), lambda b: (0, 0)),
            pl.BlockSpec((1, step * part), lambda b: (0, b)),
            pl.BlockSpec((step, units, part), lambda b: (b, 0, 0)),
            pl.BlockSpec((rows, rows), lambda b: (0, 0)),
        ],
        out_specs=pl.BlockSpec((rows, units), lambda b: (0, 0)),
        scratch_shapes=[pltpu.VMEM((rows, units), F32)],
        name="top_products",
    )(top, row_weight, head, out_full, place)


def first_parts(top, row_weight, head, pre_down, pre_up, place, blocks, step):
    rows, width = top.shape
    half, units = pre_down.shape
    part = width // blocks

    def kernel(top_ref, weight_ref, head_ref, down_ref, up_ref, place_ref, dest):
        value = jnp.concatenate([down_ref[...], up_ref[...]], axis=0).astype(F32)
        hidden = (value * jax.nn.sigmoid(value)).astype(BF16)
        placed = dot(place_ref[...].astype(BF16), hidden).astype(BF16)
        first = top_ref[...].astype(F32) + weight_ref[:, :1] * head_ref[...]
        first = first.astype(BF16)
        total = dot(placed, first, ROWS_OF_BOTH).astype(BF16)
        for b in range(step):
            dest[b] = total[:, b * part : (b + 1) * part]

    return pl.pallas_call(
        kernel,
        grid=(blocks // step,),
        out_shape=jax.ShapeDtypeStruct((blocks, units, part), BF16),
        in_specs=[
            pl.BlockSpec((rows, step * part), lambda b: (0, b)),
            pl.BlockSpec((rows, 128), lambda b: (0, 0)),
            pl.BlockSpec((1, step * part), lambda b: (0, b)),
            pl.BlockSpec((half, units), lambda b: (0, 0)),
            pl.BlockSpec((half, units), lambda b: (0, 0)),
            pl.BlockSpec((rows, rows), lambda b: (0, 0)),
        ],
        out_specs=pl.BlockSpec((step, units, part), lambda b: (b, 0, 0)),
        name="first_parts",
    )(top, row_weight, head, pre_down, pre_up, place)


def held_at(upper, lower, count):
    ring = count // 2
    if upper // ring == lower // ring:
        gap = upper - lower
        return (lower, gap - 1) if gap <= ring // 2 else (upper, ring - gap - 1)
    gap = (upper - lower) % ring
    for slot in range(ring // 2):
        if LOWER_OFFSETS[slot] % ring == gap:
            return lower, ring // 2 + slot
        if UPPER_OFFSETS[slot] % ring == gap:
            return upper, ring // 2 + slot


def chain(section, core, known, same, other):
    count, tall, units = known.shape
    lead = same.shape[2]
    rows = (tall - lead) // 2
    half = rows // 2

    def kernel(section_ref, core_ref, known_ref, same_ref, other_ref, dest, reach, grads):
        even = core_ref[0] == 0
        own = section_ref[0]

        def pre_of(layer, other):
            return jnp.concatenate(
                [
                    known_ref[layer, lead : lead + half],
                    known_ref[other, lead + half : lead + rows],
                ],
                axis=0,
            ).astype(F32)

        def coupling(upper, lower):
            at, slot = held_at(upper, lower, count)
            mine, theirs = same_ref[slot, at], other_ref[slot, at]
            return jnp.concatenate(
                [jnp.where(even, mine, theirs), jnp.where(even, theirs, mine)], axis=0
            )

        for layer in range(count):
            reach[layer] = known_ref[layer, lead + rows :].astype(F32)
        for layer in range(count - 1, -1, -1):
            pre = pre_of(layer, count - 1 - layer)
            sig = jax.nn.sigmoid(pre)
            grad_pre = (reach[layer] * sig * (1.0 + pre * (1.0 - sig))).astype(BF16)
            grads[layer] = grad_pre
            if layer > 0:
                lower = jnp.concatenate([coupling(layer, low) for low in range(layer)], axis=1)
                update = dot(grad_pre, lower)
                for low in range(layer):
                    reach[low] += update[:, low * units : (low + 1) * units]
        far = count - 1 - own
        pre = pre_of(own, far)
        hidden = (pre * jax.nn.sigmoid(pre)).astype(BF16)
        above = jnp.concatenate(
            [grads[jnp.minimum(own + up, count - 1)] for up in range(1, count)], axis=1
        )
        cross = dot(hidden, above, ROWS_OF_BOTH)
        sent = jnp.concatenate([grads[own][:half], grads[far][half:]], axis=0)
        for up in range(count):
            if up == 0:
                dest[up, :units] = jnp.zeros((units, units), BF16)
            else:
                block = cross[:, (up - 1) * units : up * units]
                dest[up, :units] = jnp.where(own + up < count, block, 0.0).astype(BF16)
            dest[up, units:] = sent

    return pl.pallas_call(
        kernel,
        out_shape=jax.ShapeDtypeStruct((count, units + rows, units), BF16),
        in_specs=[smem(), smem(), vmem(), vmem(), vmem()],
        out_specs=vmem(),
        scratch_shapes=[
            pltpu.VMEM((count, rows, units), F32),
            pltpu.VMEM((count, rows, units), BF16),
        ],
        name="chain",
    )(section, core, known, same, other)


def input_grads(wide, shared, step, side, kind):
    blocks, rows, part = wide.shape
    tall, units = shared.shape[1:]
    half = rows // 2
    skip = tall - rows + side * half

    def kernel(wide_ref, shared_ref, dest, acc):
        at = pl.program_id(0)

        @pl.when(at == 0)
        def _():
            acc[...] = jnp.zeros_like(acc)

        total = acc[...]
        for b in range(step):
            total = total + dot(shared_ref[b, skip : skip + half], wide_ref[b], ROWS_OF_BOTH)
        acc[...] = total

        @pl.when(at == pl.num_programs(0) - 1)
        def _():
            dest[...] = acc[...].astype(kind)

    return pl.pallas_call(
        kernel,
        grid=(blocks // step,),
        out_shape=jax.ShapeDtypeStruct((units, part), kind),
        in_specs=[
            pl.BlockSpec((step, half, part), lambda b: (b, side, 0)),
            pl.BlockSpec((step, tall, units), lambda b: (b, 0, 0)),
        ],
        out_specs=pl.BlockSpec((units, part), lambda b: (0, 0)),
        scratch_shapes=[pltpu.VMEM((units, part), F32)],
    )(wide, shared)


def output_grads(section, cross, first, weights):
    count, units, _ = cross.shape
    part = first.shape[1]
    ring = count // 2

    def kernel(section_ref, cross_ref, first_ref, weights_ref, dest):
        own = section_ref[0]
        upper = own >= ring
        place = jnp.where(upper, own - ring, own)
        dest[...] = first_ref[...].astype(F32)
        for z in range(ring):

            @pl.when(z > place)
            def _():
                dest[...] += dot(cross_ref[z - place], weights_ref[z, 0])

            @pl.when(jnp.logical_not(upper))
            def _():
                dest[...] += dot(cross_ref[jnp.minimum(ring + z - place, count - 1)], weights_ref[z, 1])

    return pl.pallas_call(
        kernel,
        out_shape=jax.ShapeDtypeStruct((units, part), F32),
        in_specs=[smem()] + [vmem()] * 3,
        out_specs=vmem(),
        name="output_grads",
    )(section, cross, first, weights)


def on_device(
    branch_in,
    branch_out,
    down_inputs,
    up_inputs,
    top_grads,
    plan,
    reward_pos,
    reward_cot,
    reward_head,
):
    count = lax.axis_size("section")
    blocks = lax.axis_size("fsdp")
    section_idx = lax.axis_index("section")
    fsdp_idx = lax.axis_index("fsdp")
    section = section_idx.astype(jnp.int32).reshape(1)
    _, micro, row_count, width = down_inputs.shape
    units = branch_in.shape[2]
    part = width // blocks
    half = micro * row_count
    rows = 2 * half
    step = 4

    core = (fsdp_idx % 2).astype(jnp.int32).reshape(1)
    groups = same_core(blocks)

    in_t = branch_in[0].T
    out_t = branch_out[0]
    down = down_inputs[0].reshape(half, width)
    up = up_inputs[0].reshape(half, width)
    out_full = lax.all_gather(out_t, "fsdp", axis=0)
    wide = exchanged(laid_out(down, up, blocks, step), "fsdp")
    ring = count // 2
    place_idx = section_idx % ring
    partner = lax.ppermute(
        jnp.where(section_idx >= ring, in_t, out_t),
        "section",
        [(k, (k + ring) % count) for k in range(count)],
    )
    inner, outer = [], []
    for slot in range(ring // 2):
        steps = slot + 1
        inner.append(
            inside_half(
                jnp.where(place_idx >= steps, in_t, out_t),
                steps,
                ring // 2 if 2 * steps == ring else ring,
            )
        )
    far_in_t = mirrored(in_t)
    for slot in range(ring // 2):
        outer.append(across(partner, slot))
    weights = lax.all_gather(
        jnp.stack([in_t, partner]),
        "section",
        axis=0,
        axis_index_groups=[list(range(ring)), list(range(ring, count))],
    )

    coupled = couplings(section, in_t, out_t, partner, inner, outer, count)
    coupled = coupled.reshape(blocks, -1, units)
    lead = coupled.shape[1]
    row_weight, place = row_setup(
        fsdp_idx.astype(jnp.int32).reshape(1), plan, reward_pos, reward_cot, row_count
    )
    top = top_grads.reshape(rows, width)
    head = reward_head.reshape(1, width)
    parts = pre_parts(wide, coupled, in_t, far_in_t, step)
    parts = exchanged(parts, "fsdp")
    reached = top_products(top, row_weight, head, out_full, place, step)
    known, own_pre = folded_with(parts, reached, count, lead)
    known = exchanged(known, "section")
    mirror_pre = lax.dynamic_slice_in_dim(known, count - 1 - section_idx, 1, 0)
    mirror_pre = mirror_pre[0, lead + half : lead + rows]
    firsts = first_parts(top, row_weight, head, own_pre, mirror_pre, place, blocks, step)
    first = lax.psum_scatter(
        firsts.reshape(blocks * units, part), "fsdp", scatter_dimension=0, tiled=True
    )
    coupled = known[:, :lead]
    coupled_same = exchanged(
        jnp.broadcast_to(coupled[None], (blocks // 2,) + coupled.shape), "fsdp", groups
    )
    coupled_other = from_other_core(coupled_same)

    shared = chain(section, core, known, coupled_same, coupled_other)
    shared = exchanged(shared, "fsdp")
    far_in = input_grads(wide, shared, step, 1, BF16)
    back_in = mirrored(far_in)
    cross = exchanged(folded(shared, blocks, units), "fsdp")
    own_in = input_grads(wide, shared, step, 0, F32)
    grad_out = output_grads(section, cross, first, weights)
    grad_in = (own_in + back_in.astype(F32)).T
    return (grad_in[None], grad_out[None])


def solution(mesh):
    in_specs = (
        P("section", "fsdp", None),
        P("section", None, "fsdp"),
        P("section", None, "fsdp", None),
        P("section", None, "fsdp", None),
        P(None, None, "fsdp", None),
        P(),
        P(),
        P(),
        P(),
    )
    out_specs = (P("section", "fsdp", None), P("section", None, "fsdp"))
    return jax.shard_map(
        on_device, mesh=mesh, in_specs=in_specs, out_specs=out_specs, check_vma=False
    )
```

```python
import jax
import jax.numpy as jnp
from jax import lax
from jax.experimental import pallas as pl
from jax.experimental.pallas import tpu as pltpu
from jax.sharding import PartitionSpec as P


BF16 = jnp.bfloat16
F32 = jnp.float32
ROWS_OF_BOTH = (((0,), (0,)), ((), ()))
COLS_OF_BOTH = (((1,), (1,)), ((), ()))


def dot(left, right, dims=(((1,), (0,)), ((), ()))):
    return lax.dot_general(left, right, dims, preferred_element_type=F32)


LOWER_OFFSETS = (0, -3, -1, 4)
UPPER_OFFSETS = (1, 2, 3, -2)


def inside_half(value, steps, ends):
    ring = lax.axis_size("section") // 2
    pairs = []
    for base in (0, ring):
        pairs += [(base + (z + steps) % ring, base + z) for z in range(ends)]
    return lax.ppermute(value, "section", pairs)


def across(value, slot):
    ring = lax.axis_size("section") // 2
    low, high = LOWER_OFFSETS[slot], UPPER_OFFSETS[slot]
    pairs = [(ring + (z - high) % ring, ring + z) for z in range(ring)]
    if low:
        pairs += [((z + low) % ring, z) for z in range(ring)]
    return lax.ppermute(value, "section", pairs)


def mirrored(value):
    count = lax.axis_size("section")
    return lax.ppermute(value, "section", [(k, count - 1 - k) for k in range(count)])


def exchanged(parts, axis, groups=None):
    return lax.all_to_all(parts, axis, 0, 0, axis_index_groups=groups, tiled=True)


def same_core(count):
    return [list(range(core, count, 2)) for core in range(2)]


def from_other_core(value):
    count = lax.axis_size("fsdp")
    return lax.ppermute(value, "fsdp", [(f, f ^ 1) for f in range(count)])


def vmem():
    return pl.BlockSpec(memory_space=pltpu.VMEM)


def smem():
    return pl.BlockSpec(memory_space=pltpu.SMEM)


def couplings(section, in_t, out_t, partner, inner, outer, count):
    units = in_t.shape[0]
    ring = count // 2
    slots = len(inner)

    def kernel(section_ref, in_ref, out_ref, partner_ref, *refs):
        dest = refs[2 * slots]
        own = section_ref[0]
        upper = own >= ring

        def store(slot, other, as_lower):
            @pl.when(as_lower)
            def _():
                dest[slot] = dot(other[...], out_ref[...], COLS_OF_BOTH).astype(BF16)

            @pl.when(jnp.logical_not(as_lower))
            def _():
                dest[slot] = dot(in_ref[...], other[...], COLS_OF_BOTH).astype(BF16)

        for slot in range(slots):
            store(slot, refs[slot], jnp.where(upper, own - ring, own) + slot + 1 < ring)
        for slot in range(slots):
            other = refs[slots + slot]
            if LOWER_OFFSETS[slot] == 0:

                @pl.when(upper)
                def _():
                    dest[slots + slot] = dot(in_ref[...], other[...], COLS_OF_BOTH).astype(BF16)

                @pl.when(jnp.logical_not(upper))
                def _():
                    value = dot(partner_ref[...], out_ref[...], COLS_OF_BOTH)
                    dest[slots + slot] = value.astype(BF16)
            else:
                store(slots + slot, other, jnp.logical_not(upper))

    return pl.pallas_call(
        kernel,
        out_shape=jax.ShapeDtypeStruct((2 * slots, units, units), BF16),
        in_specs=[smem()] + [vmem()] * (3 + 2 * slots),
        out_specs=vmem(),
        name="couplings",
    )(section, in_t, out_t, partner, *inner, *outer)


def laid_out(down, up, blocks, step):
    half, width = down.shape
    part = width // blocks

    def kernel(down_ref, up_ref, dest):
        for b in range(step):
            dest[b, :half] = down_ref[:, b * part : (b + 1) * part]
            dest[b, half:] = up_ref[:, b * part : (b + 1) * part]

    return pl.pallas_call(
        kernel,
        grid=(blocks // step,),
        out_shape=jax.ShapeDtypeStruct((blocks, 2 * half, part), BF16),
        in_specs=[pl.BlockSpec((half, step * part), lambda b: (0, b))] * 2,
        out_specs=pl.BlockSpec((step, 2 * half, part), lambda b: (b, 0, 0)),
        name="laid_out",
    )(down, up)


def folded(parts, copies, used):
    blocks, _, units = parts.shape

    def kernel(parts_ref, dest):
        total = parts_ref[0, :used].astype(F32)
        for b in range(1, blocks):
            total = total + parts_ref[b, :used].astype(F32)
        total = total.astype(BF16)
        for c in range(copies):
            dest[c] = total

    return pl.pallas_call(
        kernel,
        out_shape=jax.ShapeDtypeStruct((copies, used, units), BF16),
        in_specs=[vmem()],
        out_specs=vmem(),
        name="folded",
    )(parts)


def folded_with(parts, below, copies, lead):
    blocks, rows, units = parts.shape
    kept = rows - lead
    half = kept // 2

    def kernel(parts_ref, below_ref, coupled, known, far):
        total = parts_ref[0].astype(F32)
        for b in range(1, blocks):
            total = total + parts_ref[b].astype(F32)
        total = total.astype(BF16)
        for c in range(copies):
            coupled[c] = total[:lead]
        known[:kept] = total[lead:]
        known[kept:] = below_ref[...]
        far[...] = total[lead + half :]

    return pl.pallas_call(
        kernel,
        out_shape=[
            jax.ShapeDtypeStruct((copies, lead, units), BF16),
            jax.ShapeDtypeStruct((kept + below.shape[0], units), BF16),
            jax.ShapeDtypeStruct((half, units), BF16),
        ],
        in_specs=[vmem(), vmem()],
        out_specs=[vmem(), vmem(), vmem()],
        name="folded_with",
    )(parts, below)


def row_setup(fsdp, plan, reward_pos, reward_cot, row_count):
    directions, micro = plan.shape
    rows = directions * micro * row_count

    def kernel(fsdp_ref, plan_ref, pos_ref, cot_ref, weight, place):
        at = fsdp_ref[0]
        row = lax.broadcasted_iota(jnp.int32, (row_count, 128), 0)
        wide_row = lax.broadcasted_iota(jnp.int32, (row_count, rows), 0)
        wide_col = lax.broadcasted_iota(jnp.int32, (row_count, rows), 1)
        for d in range(directions):
            for j in range(micro):
                ident = plan_ref[d, j]
                base = (d * micro + j) * row_count
                spot = (d * micro + ident) * row_count
                value = jnp.where(row == pos_ref[d, ident, at], cot_ref[d, ident, at], 0.0)
                weight[base : base + row_count] = value
                place[base : base + row_count] = jnp.where(
                    wide_col == wide_row + spot, 1.0, 0.0
                )

    return pl.pallas_call(
        kernel,
        out_shape=[
            jax.ShapeDtypeStruct((rows, 128), F32),
            jax.ShapeDtypeStruct((rows, rows), F32),
        ],
        in_specs=[smem()] * 4,
        out_specs=[vmem(), vmem()],
        name="row_setup",
    )(fsdp, plan, reward_pos, reward_cot)


def pre_parts(wide, coupled, in_t, far_in_t, step):
    blocks, rows, part = wide.shape
    units = in_t.shape[0]
    lead = coupled.shape[1]
    half = rows // 2

    def kernel(wide_ref, coupled_ref, in_ref, far_ref, dest):
        for b in range(step):
            dest[b, :lead] = coupled_ref[b]
            dest[b, lead : lead + half] = dot(
                wide_ref[b, :half], in_ref[...], COLS_OF_BOTH
            ).astype(BF16)
            dest[b, lead + half :] = dot(
                wide_ref[b, half:], far_ref[...], COLS_OF_BOTH
            ).astype(BF16)

    return pl.pallas_call(
        kernel,
        grid=(blocks // step,),
        out_shape=jax.ShapeDtypeStruct((blocks, lead + rows, units), BF16),
        in_specs=[
            pl.BlockSpec((step, rows, part), lambda b: (b, 0, 0)),
            pl.BlockSpec((step, lead, units), lambda b: (b, 0, 0)),
            pl.BlockSpec((units, part), lambda b: (0, 0)),
            pl.BlockSpec((units, part), lambda b: (0, 0)),
        ],
        out_specs=pl.BlockSpec((step, lead + rows, units), lambda b: (b, 0, 0)),
        name="pre_parts",
    )(wide, coupled, in_t, far_in_t)


def top_products(top, row_weight, head, out_full, place, step):
    blocks, units, part = out_full.shape
    rows = top.shape[0]

    def kernel(top_ref, weight_ref, head_ref, out_ref, place_ref, dest, acc):
        at = pl.program_id(0)

        @pl.when(at == 0)
        def _():
            acc[...] = jnp.zeros_like(acc)

        first = top_ref[...].astype(F32) + weight_ref[:, :1] * head_ref[...]
        first = first.astype(BF16)
        total = acc[...]
        for b in range(step):
            total = total + dot(first[:, b * part : (b + 1) * part], out_ref[b], COLS_OF_BOTH)
        acc[...] = total

        @pl.when(at == pl.num_programs(0) - 1)
        def _():
            dest[...] = dot(
                place_ref[...].astype(BF16), acc[...].astype(BF16), ROWS_OF_BOTH
            ).astype(BF16)

    return pl.pallas_call(
        kernel,
        grid=(blocks // step,),
        out_shape=jax.ShapeDtypeStruct((rows, units), BF16),
        in_specs=[
            pl.BlockSpec((rows, step * part), lambda b: (0, b)),
            pl.BlockSpec((rows, 128), lambda b: (0, 0)),
            pl.BlockSpec((1, step * part), lambda b: (0, b)),
            pl.BlockSpec((step, units, part), lambda b: (b, 0, 0)),
            pl.BlockSpec((rows, rows), lambda b: (0, 0)),
        ],
        out_specs=pl.BlockSpec((rows, units), lambda b: (0, 0)),
        scratch_shapes=[pltpu.VMEM((rows, units), F32)],
        name="top_products",
    )(top, row_weight, head, out_full, place)


def first_parts(top, row_weight, head, pre_down, pre_up, place, blocks, step):
    rows, width = top.shape
    half, units = pre_up.shape
    part = width // blocks

    def kernel(top_ref, weight_ref, head_ref, down_ref, up_ref, place_ref, dest):
        value = jnp.concatenate([down_ref[:half], up_ref[...]], axis=0).astype(F32)
        hidden = (value * jax.nn.sigmoid(value)).astype(BF16)
        placed = dot(place_ref[...].astype(BF16), hidden).astype(BF16)
        first = top_ref[...].astype(F32) + weight_ref[:, :1] * head_ref[...]
        first = first.astype(BF16)
        total = dot(placed, first, ROWS_OF_BOTH).astype(BF16)
        for b in range(step):
            dest[b] = total[:, b * part : (b + 1) * part]

    return pl.pallas_call(
        kernel,
        grid=(blocks // step,),
        out_shape=jax.ShapeDtypeStruct((blocks, units, part), BF16),
        in_specs=[
            pl.BlockSpec((rows, step * part), lambda b: (0, b)),
            pl.BlockSpec((rows, 128), lambda b: (0, 0)),
            pl.BlockSpec((1, step * part), lambda b: (0, b)),
            pl.BlockSpec((2 * rows, units), lambda b: (0, 0)),
            pl.BlockSpec((half, units), lambda b: (0, 0)),
            pl.BlockSpec((rows, rows), lambda b: (0, 0)),
        ],
        out_specs=pl.BlockSpec((step, units, part), lambda b: (b, 0, 0)),
        name="first_parts",
    )(top, row_weight, head, pre_down, pre_up, place)


def held_at(upper, lower, count):
    ring = count // 2
    if upper // ring == lower // ring:
        gap = upper - lower
        return (lower, gap - 1) if gap <= ring // 2 else (upper, ring - gap - 1)
    gap = (upper - lower) % ring
    for slot in range(ring // 2):
        if LOWER_OFFSETS[slot] % ring == gap:
            return lower, ring // 2 + slot
        if UPPER_OFFSETS[slot] % ring == gap:
            return upper, ring // 2 + slot


def chain(section, core, held, same, other, count):
    ring = count // 2
    _, tall, units = held[0].shape
    rows = tall // 2
    half = rows // 2

    def kernel(section_ref, core_ref, same_ref, other_ref, *refs):
        dest, known_ref, reach, grads = refs[ring:]
        even = core_ref[0] == 0
        own = section_ref[0]
        base = jnp.where(own >= ring, ring, 0)
        for steps in range(ring):
            at = lax.rem(own - base + steps, ring)
            known_ref[base + at] = refs[steps][0]
            known_ref[ring - base + at] = refs[steps][1]

        def pre_of(layer, other):
            return jnp.concatenate(
                [
                    known_ref[layer, :half],
                    known_ref[other, half:rows],
                ],
                axis=0,
            ).astype(F32)

        def coupling(upper, lower):
            at, slot = held_at(upper, lower, count)
            mine, theirs = same_ref[slot, at], other_ref[slot, at]
            return jnp.concatenate(
                [jnp.where(even, mine, theirs), jnp.where(even, theirs, mine)], axis=0
            )

        for layer in range(count):
            reach[layer] = known_ref[layer, rows:].astype(F32)
        for layer in range(count - 1, -1, -1):
            pre = pre_of(layer, count - 1 - layer)
            sig = jax.nn.sigmoid(pre)
            grad_pre = (reach[layer] * sig * (1.0 + pre * (1.0 - sig))).astype(BF16)
            grads[layer] = grad_pre
            if layer > 0:
                lower = jnp.concatenate([coupling(layer, low) for low in range(layer)], axis=1)
                update = dot(grad_pre, lower)
                for low in range(layer):
                    reach[low] += update[:, low * units : (low + 1) * units]
        far = count - 1 - own
        pre = pre_of(own, far)
        hidden = (pre * jax.nn.sigmoid(pre)).astype(BF16)
        above = jnp.concatenate(
            [grads[jnp.minimum(own + up, count - 1)] for up in range(1, count)], axis=1
        )
        cross = dot(hidden, above, ROWS_OF_BOTH)
        sent = jnp.concatenate([grads[own][:half], grads[far][half:]], axis=0)
        for up in range(count):
            if up == 0:
                dest[up, :units] = jnp.zeros((units, units), BF16)
            else:
                block = cross[:, (up - 1) * units : up * units]
                dest[up, :units] = jnp.where(own + up < count, block, 0.0).astype(BF16)
            dest[up, units:] = sent

    return pl.pallas_call(
        kernel,
        out_shape=jax.ShapeDtypeStruct((count, units + rows, units), BF16),
        in_specs=[smem(), smem()] + [vmem()] * (2 + ring),
        out_specs=vmem(),
        scratch_shapes=[
            pltpu.VMEM((count, tall, units), BF16),
            pltpu.VMEM((count, rows, units), F32),
            pltpu.VMEM((count, rows, units), BF16),
        ],
        name="chain",
    )(section, core, same, other, *held)


def input_grads(wide, shared, step, side, kind):
    blocks, rows, part = wide.shape
    tall, units = shared.shape[1:]
    half = rows // 2
    skip = tall - rows + side * half

    def kernel(wide_ref, shared_ref, dest, acc):
        at = pl.program_id(0)

        @pl.when(at == 0)
        def _():
            acc[...] = jnp.zeros_like(acc)

        total = acc[...]
        for b in range(step):
            total = total + dot(shared_ref[b, skip : skip + half], wide_ref[b], ROWS_OF_BOTH)
        acc[...] = total

        @pl.when(at == pl.num_programs(0) - 1)
        def _():
            dest[...] = acc[...].astype(kind)

    return pl.pallas_call(
        kernel,
        grid=(blocks // step,),
        out_shape=jax.ShapeDtypeStruct((units, part), kind),
        in_specs=[
            pl.BlockSpec((step, half, part), lambda b: (b, side, 0)),
            pl.BlockSpec((step, tall, units), lambda b: (b, 0, 0)),
        ],
        out_specs=pl.BlockSpec((units, part), lambda b: (0, 0)),
        scratch_shapes=[pltpu.VMEM((units, part), F32)],
    )(wide, shared)


def output_grads(section, cross, first, weights):
    count, units, _ = cross.shape
    part = first.shape[1]
    ring = count // 2

    def kernel(section_ref, cross_ref, first_ref, weights_ref, dest):
        own = section_ref[0]
        upper = own >= ring
        place = jnp.where(upper, own - ring, own)
        dest[...] = first_ref[...].astype(F32)
        for z in range(ring):

            @pl.when(z > place)
            def _():
                dest[...] += dot(cross_ref[z - place], weights_ref[z, 0])

            @pl.when(jnp.logical_not(upper))
            def _():
                dest[...] += dot(cross_ref[jnp.minimum(ring + z - place, count - 1)], weights_ref[z, 1])

    return pl.pallas_call(
        kernel,
        out_shape=jax.ShapeDtypeStruct((units, part), F32),
        in_specs=[smem()] + [vmem()] * 3,
        out_specs=vmem(),
        name="output_grads",
    )(section, cross, first, weights)


def on_device(
    branch_in,
    branch_out,
    down_inputs,
    up_inputs,
    top_grads,
    plan,
    reward_pos,
    reward_cot,
    reward_head,
):
    count = lax.axis_size("section")
    blocks = lax.axis_size("fsdp")
    section_idx = lax.axis_index("section")
    fsdp_idx = lax.axis_index("fsdp")
    section = section_idx.astype(jnp.int32).reshape(1)
    _, micro, row_count, width = down_inputs.shape
    units = branch_in.shape[2]
    part = width // blocks
    half = micro * row_count
    rows = 2 * half
    step = 4

    core = (fsdp_idx % 2).astype(jnp.int32).reshape(1)
    groups = same_core(blocks)

    in_t = branch_in[0].T
    out_t = branch_out[0]
    down = down_inputs[0].reshape(half, width)
    up = up_inputs[0].reshape(half, width)
    out_full = lax.all_gather(out_t, "fsdp", axis=0)
    wide = exchanged(laid_out(down, up, blocks, step), "fsdp")
    ring = count // 2
    place_idx = section_idx % ring
    partner = lax.ppermute(
        jnp.where(section_idx >= ring, in_t, out_t),
        "section",
        [(k, (k + ring) % count) for k in range(count)],
    )
    inner, outer = [], []
    for slot in range(ring // 2):
        steps = slot + 1
        inner.append(
            inside_half(
                jnp.where(place_idx >= steps, in_t, out_t),
                steps,
                ring // 2 if 2 * steps == ring else ring,
            )
        )
    far_in_t = mirrored(in_t)
    for slot in range(ring // 2):
        outer.append(across(partner, slot))
    weights = lax.all_gather(
        jnp.stack([in_t, partner]),
        "section",
        axis=0,
        axis_index_groups=[list(range(ring)), list(range(ring, count))],
    )

    coupled = couplings(section, in_t, out_t, partner, inner, outer, count)
    coupled = coupled.reshape(blocks, -1, units)
    lead = coupled.shape[1]
    row_weight, place = row_setup(
        fsdp_idx.astype(jnp.int32).reshape(1), plan, reward_pos, reward_cot, row_count
    )
    top = top_grads.reshape(rows, width)
    head = reward_head.reshape(1, width)
    parts = pre_parts(wide, coupled, in_t, far_in_t, step)
    parts = exchanged(parts, "fsdp")
    reached = top_products(top, row_weight, head, out_full, place, step)
    coupled, known, far_pre = folded_with(parts, reached, count, lead)
    coupled = exchanged(coupled, "section")
    mirror_pre = mirrored(far_pre)
    known_partner = lax.ppermute(known, "section", [(k, (k + ring) % count) for k in range(count)])
    held = [jnp.stack([known, known_partner])]
    for steps in range(1, ring):
        held.append(inside_half(held[0], steps, ring))
    firsts = first_parts(top, row_weight, head, known, mirror_pre, place, blocks, step)
    first = lax.psum_scatter(
        firsts.reshape(blocks * units, part), "fsdp", scatter_dimension=0, tiled=True
    )
    coupled_same = exchanged(
        jnp.broadcast_to(coupled[None], (blocks // 2,) + coupled.shape), "fsdp", groups
    )
    coupled_other = from_other_core(coupled_same)

    shared = chain(section, core, held, coupled_same, coupled_other, count)
    shared = exchanged(shared, "fsdp")
    far_in = input_grads(wide, shared, step, 1, BF16)
    back_in = mirrored(far_in)
    cross = exchanged(folded(shared, blocks, units), "fsdp")
    own_in = input_grads(wide, shared, step, 0, F32)
    grad_out = output_grads(section, cross, first, weights)
    grad_in = (own_in + back_in.astype(F32)).T
    return (grad_in[None], grad_out[None])


def solution(mesh):
    in_specs = (
        P("section", "fsdp", None),
        P("section", None, "fsdp"),
        P("section", None, "fsdp", None),
        P("section", None, "fsdp", None),
        P(None, None, "fsdp", None),
        P(),
        P(),
        P(),
        P(),
    )
    out_specs = (P("section", "fsdp", None), P("section", None, "fsdp"))
    return jax.shard_map(
        on_device, mesh=mesh, in_specs=in_specs, out_specs=out_specs, check_vma=False
    )
```

```python
import jax
import jax.numpy as jnp
from jax import lax
from jax.experimental import pallas as pl
from jax.experimental.pallas import tpu as pltpu
from jax.sharding import PartitionSpec as P


BF16 = jnp.bfloat16
F32 = jnp.float32
ROWS_OF_BOTH = (((0,), (0,)), ((), ()))
COLS_OF_BOTH = (((1,), (1,)), ((), ()))


def dot(left, right, dims=(((1,), (0,)), ((), ()))):
    return lax.dot_general(left, right, dims, preferred_element_type=F32)


LOWER_OFFSETS = (0, -3, -1, 4)
UPPER_OFFSETS = (1, 2, 3, -2)


def inside_half(value, steps, ends):
    ring = lax.axis_size("section") // 2
    pairs = []
    for base in (0, ring):
        pairs += [(base + (z + steps) % ring, base + z) for z in range(ends)]
    return lax.ppermute(value, "section", pairs)


def across(value, slot):
    ring = lax.axis_size("section") // 2
    low, high = LOWER_OFFSETS[slot], UPPER_OFFSETS[slot]
    pairs = [(ring + (z - high) % ring, ring + z) for z in range(ring)]
    if low:
        pairs += [((z + low) % ring, z) for z in range(ring)]
    return lax.ppermute(value, "section", pairs)


def mirrored(value):
    count = lax.axis_size("section")
    return lax.ppermute(value, "section", [(k, count - 1 - k) for k in range(count)])


def upward(value, steps):
    ring = lax.axis_size("section") // 2
    pairs = []
    for base in (0, ring):
        pairs += [(base + z + steps, base + z) for z in range(ring - steps)]
    return lax.ppermute(value, "section", pairs)


def lower_only(value, steps):
    ring = lax.axis_size("section") // 2
    return lax.ppermute(value, "section", [((z + steps) % ring, z) for z in range(ring)])


def between_chips(value, mask):
    count = lax.axis_size("fsdp")
    return lax.ppermute(value, "fsdp", [(f, f ^ (2 * mask)) for f in range(count)])


def exchanged(parts, axis, groups=None):
    return lax.all_to_all(parts, axis, 0, 0, axis_index_groups=groups, tiled=True)


def same_core(count):
    return [list(range(core, count, 2)) for core in range(2)]


def from_other_core(value):
    count = lax.axis_size("fsdp")
    return lax.ppermute(value, "fsdp", [(f, f ^ 1) for f in range(count)])


def vmem():
    return pl.BlockSpec(memory_space=pltpu.VMEM)


def smem():
    return pl.BlockSpec(memory_space=pltpu.SMEM)


def couplings(section, in_t, out_t, partner, inner, outer, count):
    units = in_t.shape[0]
    ring = count // 2
    slots = len(inner)

    def kernel(section_ref, in_ref, out_ref, partner_ref, *refs):
        dest = refs[2 * slots]
        own = section_ref[0]
        upper = own >= ring

        def store(slot, other, as_lower):
            @pl.when(as_lower)
            def _():
                dest[slot] = dot(other[...], out_ref[...], COLS_OF_BOTH).astype(BF16)

            @pl.when(jnp.logical_not(as_lower))
            def _():
                dest[slot] = dot(in_ref[...], other[...], COLS_OF_BOTH).astype(BF16)

        for slot in range(slots):
            store(slot, refs[slot], jnp.where(upper, own - ring, own) + slot + 1 < ring)
        for slot in range(slots):
            other = refs[slots + slot]
            if LOWER_OFFSETS[slot] == 0:

                @pl.when(upper)
                def _():
                    dest[slots + slot] = dot(in_ref[...], other[...], COLS_OF_BOTH).astype(BF16)

                @pl.when(jnp.logical_not(upper))
                def _():
                    value = dot(partner_ref[...], out_ref[...], COLS_OF_BOTH)
                    dest[slots + slot] = value.astype(BF16)
            else:
                store(slots + slot, other, jnp.logical_not(upper))

    return pl.pallas_call(
        kernel,
        out_shape=jax.ShapeDtypeStruct((2 * slots, units, units), BF16),
        in_specs=[smem()] + [vmem()] * (3 + 2 * slots),
        out_specs=vmem(),
        name="couplings",
    )(section, in_t, out_t, partner, *inner, *outer)


def laid_out(down, up, blocks, step):
    half, width = down.shape
    part = width // blocks

    def kernel(down_ref, up_ref, dest):
        for b in range(step):
            dest[b, :half] = down_ref[:, b * part : (b + 1) * part]
            dest[b, half:] = up_ref[:, b * part : (b + 1) * part]

    return pl.pallas_call(
        kernel,
        grid=(blocks // step,),
        out_shape=jax.ShapeDtypeStruct((blocks, 2 * half, part), BF16),
        in_specs=[pl.BlockSpec((half, step * part), lambda b: (0, b))] * 2,
        out_specs=pl.BlockSpec((step, 2 * half, part), lambda b: (b, 0, 0)),
        name="laid_out",
    )(down, up)


def stacked(pieces):
    count = len(pieces)

    def kernel(*refs):
        for at in range(count):
            refs[count][at] = refs[at][...]

    return pl.pallas_call(
        kernel,
        out_shape=jax.ShapeDtypeStruct((count,) + pieces[0].shape, BF16),
        in_specs=[vmem()] * count,
        out_specs=vmem(),
        name="stacked",
    )(*pieces)


def added(kept, received):
    count = kept.shape[0]

    def kernel(kept_ref, received_ref, *dests):
        for at in range(count):
            total = kept_ref[at].astype(F32) + received_ref[at].astype(F32)
            dests[at][...] = total.astype(BF16)

    return pl.pallas_call(
        kernel,
        out_shape=[jax.ShapeDtypeStruct(kept.shape[1:], BF16)] * count,
        in_specs=[vmem(), vmem()],
        out_specs=[vmem()] * count,
        name="added",
    )(kept, received)


def folded(parts, copies, used):
    blocks, _, units = parts.shape

    def kernel(parts_ref, dest):
        total = parts_ref[0, :used].astype(F32)
        for b in range(1, blocks):
            total = total + parts_ref[b, :used].astype(F32)
        total = total.astype(BF16)
        for c in range(copies):
            dest[c] = total

    return pl.pallas_call(
        kernel,
        out_shape=jax.ShapeDtypeStruct((copies, used, units), BF16),
        in_specs=[vmem()],
        out_specs=vmem(),
        name="folded",
    )(parts)


def folded_with(parts, below, copies, lead):
    blocks, rows, units = parts.shape
    kept = rows - lead
    half = kept // 2

    def kernel(parts_ref, below_ref, coupled, known, far):
        total = parts_ref[0].astype(F32)
        for b in range(1, blocks):
            total = total + parts_ref[b].astype(F32)
        total = total.astype(BF16)
        for c in range(copies):
            coupled[c] = total[:lead]
        known[:kept] = total[lead:]
        known[kept:] = below_ref[...]
        far[...] = total[lead + half :]

    return pl.pallas_call(
        kernel,
        out_shape=[
            jax.ShapeDtypeStruct((copies, lead, units), BF16),
            jax.ShapeDtypeStruct((kept + below.shape[0], units), BF16),
            jax.ShapeDtypeStruct((half, units), BF16),
        ],
        in_specs=[vmem(), vmem()],
        out_specs=[vmem(), vmem(), vmem()],
        name="folded_with",
    )(parts, below)


def row_setup(fsdp, plan, reward_pos, reward_cot, row_count):
    directions, micro = plan.shape
    rows = directions * micro * row_count

    def kernel(fsdp_ref, plan_ref, pos_ref, cot_ref, weight, place):
        at = fsdp_ref[0]
        row = lax.broadcasted_iota(jnp.int32, (row_count, 128), 0)
        wide_row = lax.broadcasted_iota(jnp.int32, (row_count, rows), 0)
        wide_col = lax.broadcasted_iota(jnp.int32, (row_count, rows), 1)
        for d in range(directions):
            for j in range(micro):
                ident = plan_ref[d, j]
                base = (d * micro + j) * row_count
                spot = (d * micro + ident) * row_count
                value = jnp.where(row == pos_ref[d, ident, at], cot_ref[d, ident, at], 0.0)
                weight[base : base + row_count] = value
                place[base : base + row_count] = jnp.where(
                    wide_col == wide_row + spot, 1.0, 0.0
                )

    return pl.pallas_call(
        kernel,
        out_shape=[
            jax.ShapeDtypeStruct((rows, 128), F32),
            jax.ShapeDtypeStruct((rows, rows), F32),
        ],
        in_specs=[smem()] * 4,
        out_specs=[vmem(), vmem()],
        name="row_setup",
    )(fsdp, plan, reward_pos, reward_cot)


def pre_parts(wide, coupled, in_t, far_in_t, step):
    blocks, rows, part = wide.shape
    units = in_t.shape[0]
    lead = coupled.shape[1]
    half = rows // 2

    def kernel(wide_ref, coupled_ref, in_ref, far_ref, dest):
        for b in range(step):
            dest[b, :lead] = coupled_ref[b]
            dest[b, lead : lead + half] = dot(
                wide_ref[b, :half], in_ref[...], COLS_OF_BOTH
            ).astype(BF16)
            dest[b, lead + half :] = dot(
                wide_ref[b, half:], far_ref[...], COLS_OF_BOTH
            ).astype(BF16)

    return pl.pallas_call(
        kernel,
        grid=(blocks // step,),
        out_shape=jax.ShapeDtypeStruct((blocks, lead + rows, units), BF16),
        in_specs=[
            pl.BlockSpec((step, rows, part), lambda b: (b, 0, 0)),
            pl.BlockSpec((step, lead, units), lambda b: (b, 0, 0)),
            pl.BlockSpec((units, part), lambda b: (0, 0)),
            pl.BlockSpec((units, part), lambda b: (0, 0)),
        ],
        out_specs=pl.BlockSpec((step, lead + rows, units), lambda b: (b, 0, 0)),
        name="pre_parts",
    )(wide, coupled, in_t, far_in_t)


def chip_columns(rows, part, flip):
    def index(m, spot):
        core = 1 - spot[1] if flip else spot[1]
        return (0, 2 * jnp.bitwise_xor(spot[0], m) + core)

    return pl.BlockSpec((rows, part), index)


def top_products(spot, top, row_weight, head, out_same, out_other, place):
    chips, units, part = out_same.shape
    rows = top.shape[0]

    def kernel(spot_ref, top0, top1, head0, head1, weight_ref, out0, out1, place_ref, dest, acc):
        at = pl.program_id(0)

        @pl.when(at == 0)
        def _():
            acc[...] = jnp.zeros_like(acc)

        total = acc[...]
        for top_ref, head_ref, out_ref in ((top0, head0, out0), (top1, head1, out1)):
            first = top_ref[...].astype(F32) + weight_ref[:, :1] * head_ref[...]
            total = total + dot(first.astype(BF16), out_ref[0], COLS_OF_BOTH)
        acc[...] = total

        @pl.when(at == pl.num_programs(0) - 1)
        def _():
            dest[...] = dot(
                place_ref[...].astype(BF16), acc[...].astype(BF16), ROWS_OF_BOTH
            ).astype(BF16)

    return pl.pallas_call(
        kernel,
        grid_spec=pltpu.PrefetchScalarGridSpec(
            num_scalar_prefetch=1,
            grid=(chips,),
            in_specs=[
                chip_columns(rows, part, False),
                chip_columns(rows, part, True),
                chip_columns(1, part, False),
                chip_columns(1, part, True),
                pl.BlockSpec((rows, 128), lambda m, spot: (0, 0)),
                pl.BlockSpec((1, units, part), lambda m, spot: (m, 0, 0)),
                pl.BlockSpec((1, units, part), lambda m, spot: (m, 0, 0)),
                pl.BlockSpec((rows, rows), lambda m, spot: (0, 0)),
            ],
            out_specs=pl.BlockSpec((rows, units), lambda m, spot: (0, 0)),
            scratch_shapes=[pltpu.VMEM((rows, units), F32)],
        ),
        out_shape=jax.ShapeDtypeStruct((rows, units), BF16),
        name="top_products",
    )(spot, top, top, head, head, row_weight, out_same, out_other, place)


def first_parts(spot, top, row_weight, head, pre_down, pre_up, place, chips):
    rows, width = top.shape
    half, units = pre_up.shape
    part = width // (2 * chips)

    def kernel(
        spot_ref, top0, top1, head0, head1, weight_ref, down_ref, up_ref, place_ref, kept, sent, at
    ):
        @pl.when(pl.program_id(0) == 0)
        def _():
            value = jnp.concatenate([down_ref[:half], up_ref[...]], axis=0).astype(F32)
            hidden = (value * jax.nn.sigmoid(value)).astype(BF16)
            at[...] = dot(place_ref[...].astype(BF16), hidden).astype(BF16)

        for top_ref, head_ref, dest in ((top0, head0, kept), (top1, head1, sent)):
            first = top_ref[...].astype(F32) + weight_ref[:, :1] * head_ref[...]
            dest[0] = dot(at[...], first.astype(BF16), ROWS_OF_BOTH).astype(BF16)

    return pl.pallas_call(
        kernel,
        grid_spec=pltpu.PrefetchScalarGridSpec(
            num_scalar_prefetch=1,
            grid=(chips,),
            in_specs=[
                chip_columns(rows, part, False),
                chip_columns(rows, part, True),
                chip_columns(1, part, False),
                chip_columns(1, part, True),
                pl.BlockSpec((rows, 128), lambda m, spot: (0, 0)),
                pl.BlockSpec((2 * rows, units), lambda m, spot: (0, 0)),
                pl.BlockSpec((half, units), lambda m, spot: (0, 0)),
                pl.BlockSpec((rows, rows), lambda m, spot: (0, 0)),
            ],
            out_specs=[
                pl.BlockSpec((1, units, part), lambda m, spot: (m, 0, 0)),
                pl.BlockSpec((1, units, part), lambda m, spot: (m, 0, 0)),
            ],
            scratch_shapes=[pltpu.VMEM((rows, units), BF16)],
        ),
        out_shape=[jax.ShapeDtypeStruct((chips, units, part), BF16)] * 2,
        name="first_parts",
    )(spot, top, top, head, head, row_weight, pre_down, pre_up, place)


def held_at(upper, lower, count):
    ring = count // 2
    if upper // ring == lower // ring:
        gap = upper - lower
        return (lower, gap - 1) if gap <= ring // 2 else (upper, ring - gap - 1)
    gap = (upper - lower) % ring
    for slot in range(ring // 2):
        if LOWER_OFFSETS[slot] % ring == gap:
            return lower, ring // 2 + slot
        if UPPER_OFFSETS[slot] % ring == gap:
            return upper, ring // 2 + slot


def chain(section, core, held, same, other, count):
    ring = count // 2
    _, tall, units = held[0].shape
    rows = tall // 2
    half = rows // 2

    def kernel(section_ref, core_ref, same_ref, other_ref, *refs):
        dest, known_ref, reach, grads = refs[ring:]
        even = core_ref[0] == 0
        own = section_ref[0]
        base = jnp.where(own >= ring, ring, 0)
        for steps in range(ring):
            at = lax.rem(own - base + steps, ring)
            known_ref[base + at] = refs[steps][0]
            known_ref[ring - base + at] = refs[steps][1]

        def pre_of(layer, other):
            return jnp.concatenate(
                [
                    known_ref[layer, :half],
                    known_ref[other, half:rows],
                ],
                axis=0,
            ).astype(F32)

        def coupling(upper, lower):
            at, slot = held_at(upper, lower, count)
            mine, theirs = same_ref[slot, at], other_ref[slot, at]
            return jnp.concatenate(
                [jnp.where(even, mine, theirs), jnp.where(even, theirs, mine)], axis=0
            )

        for layer in range(count):
            reach[layer] = known_ref[layer, rows:].astype(F32)
        for layer in range(count - 1, -1, -1):
            pre = pre_of(layer, count - 1 - layer)
            sig = jax.nn.sigmoid(pre)
            grad_pre = (reach[layer] * sig * (1.0 + pre * (1.0 - sig))).astype(BF16)
            grads[layer] = grad_pre
            if layer > 0:
                lower = jnp.concatenate([coupling(layer, low) for low in range(layer)], axis=1)
                update = dot(grad_pre, lower)
                for low in range(layer):
                    reach[low] += update[:, low * units : (low + 1) * units]
        far = count - 1 - own
        pre = pre_of(own, far)
        hidden = (pre * jax.nn.sigmoid(pre)).astype(BF16)
        above = jnp.concatenate(
            [grads[jnp.minimum(own + up, count - 1)] for up in range(1, count)], axis=1
        )
        cross = dot(hidden, above, ROWS_OF_BOTH)
        sent = jnp.concatenate([grads[own][:half], grads[far][half:]], axis=0)
        for up in range(count):
            if up == 0:
                dest[up, :units] = jnp.zeros((units, units), BF16)
            else:
                block = cross[:, (up - 1) * units : up * units]
                dest[up, :units] = jnp.where(own + up < count, block, 0.0).astype(BF16)
            dest[up, units:] = sent

    return pl.pallas_call(
        kernel,
        out_shape=jax.ShapeDtypeStruct((count, units + rows, units), BF16),
        in_specs=[smem(), smem()] + [vmem()] * (2 + ring),
        out_specs=vmem(),
        scratch_shapes=[
            pltpu.VMEM((count, tall, units), BF16),
            pltpu.VMEM((count, rows, units), F32),
            pltpu.VMEM((count, rows, units), BF16),
        ],
        name="chain",
    )(section, core, same, other, *held)


def input_grads(wide, shared, step, side, kind):
    blocks, rows, part = wide.shape
    tall, units = shared.shape[1:]
    half = rows // 2
    skip = tall - rows + side * half

    def kernel(wide_ref, shared_ref, dest, acc):
        at = pl.program_id(0)

        @pl.when(at == 0)
        def _():
            acc[...] = jnp.zeros_like(acc)

        total = acc[...]
        for b in range(step):
            total = total + dot(shared_ref[b, skip : skip + half], wide_ref[b], ROWS_OF_BOTH)
        acc[...] = total

        @pl.when(at == pl.num_programs(0) - 1)
        def _():
            dest[...] = acc[...].astype(kind)

    return pl.pallas_call(
        kernel,
        grid=(blocks // step,),
        out_shape=jax.ShapeDtypeStruct((units, part), kind),
        in_specs=[
            pl.BlockSpec((step, half, part), lambda b: (b, side, 0)),
            pl.BlockSpec((step, tall, units), lambda b: (b, 0, 0)),
        ],
        out_specs=pl.BlockSpec((units, part), lambda b: (0, 0)),
        scratch_shapes=[pltpu.VMEM((units, part), F32)],
    )(wide, shared)


def output_grads(section, cross, firsts, inner, outer):
    count, units, _ = cross.shape
    part = firsts[0].shape[1]
    ring = count // 2
    terms = len(firsts)

    def kernel(section_ref, cross_ref, *refs):
        dest = refs[-1]
        own = section_ref[0]
        upper = own >= ring
        place = jnp.where(upper, own - ring, own)
        total = refs[0][...].astype(F32)
        for at in range(1, terms):
            total = total + refs[at][...].astype(F32)
        dest[...] = total
        for steps in range(1, ring):

            @pl.when(place + steps < ring)
            def _():
                dest[...] += dot(cross_ref[steps], refs[terms + steps - 1][...])

        for steps in range(ring):

            @pl.when(jnp.logical_not(upper))
            def _():
                at = ring + lax.rem(place + steps, ring) - place
                dest[...] += dot(cross_ref[at], refs[terms + ring - 1 + steps][...])

    return pl.pallas_call(
        kernel,
        out_shape=jax.ShapeDtypeStruct((units, part), F32),
        in_specs=[smem()] + [vmem()] * (1 + terms + len(inner) + len(outer)),
        out_specs=vmem(),
        name="output_grads",
    )(section, cross, *firsts, *inner, *outer)


def on_device(
    branch_in,
    branch_out,
    down_inputs,
    up_inputs,
    top_grads,
    plan,
    reward_pos,
    reward_cot,
    reward_head,
):
    count = lax.axis_size("section")
    blocks = lax.axis_size("fsdp")
    section_idx = lax.axis_index("section")
    fsdp_idx = lax.axis_index("fsdp")
    section = section_idx.astype(jnp.int32).reshape(1)
    _, micro, row_count, width = down_inputs.shape
    units = branch_in.shape[2]
    half = micro * row_count
    rows = 2 * half
    step = 4

    core = (fsdp_idx % 2).astype(jnp.int32).reshape(1)
    groups = same_core(blocks)

    in_t = branch_in[0].T
    out_t = branch_out[0]
    down = down_inputs[0].reshape(half, width)
    up = up_inputs[0].reshape(half, width)
    wide = exchanged(laid_out(down, up, blocks, step), "fsdp")
    ring = count // 2
    place_idx = section_idx % ring
    partner = lax.ppermute(
        jnp.where(section_idx >= ring, in_t, out_t),
        "section",
        [(k, (k + ring) % count) for k in range(count)],
    )
    inner, outer = [], []
    for slot in range(ring // 2):
        steps = slot + 1
        inner.append(
            inside_half(
                jnp.where(place_idx >= steps, in_t, out_t),
                steps,
                ring // 2 if 2 * steps == ring else ring,
            )
        )
    far_in_t = mirrored(in_t)
    for slot in range(ring // 2):
        outer.append(across(partner, slot))
    chips = blocks // 2
    spot = jnp.stack([fsdp_idx // 2, fsdp_idx % 2]).astype(jnp.int32)
    pieces = [out_t]
    for mask in range(1, chips):
        pieces.append(between_chips(out_t, mask))
    out_same = stacked(pieces)
    out_other = from_other_core(out_same)
    inner_all = list(inner)
    for steps in range(ring // 2 + 1, ring):
        inner_all.append(upward(in_t, steps))
    outer_all = []
    for steps in range(ring):
        held = [slot for slot in range(ring // 2) if LOWER_OFFSETS[slot] % ring == steps]
        if steps == 0:
            outer_all.append(partner)
        elif held:
            outer_all.append(outer[held[0]])
        else:
            outer_all.append(lower_only(partner, steps))

    coupled = couplings(section, in_t, out_t, partner, inner, outer, count)
    coupled = coupled.reshape(blocks, -1, units)
    lead = coupled.shape[1]
    row_weight, place = row_setup(
        fsdp_idx.astype(jnp.int32).reshape(1), plan, reward_pos, reward_cot, row_count
    )
    top = top_grads.reshape(rows, width)
    head = reward_head.reshape(1, width)
    parts = pre_parts(wide, coupled, in_t, far_in_t, step)
    parts = exchanged(parts, "fsdp")
    reached = top_products(spot, top, row_weight, head, out_same, out_other, place)
    coupled, known, far_pre = folded_with(parts, reached, count, lead)
    coupled = exchanged(coupled, "section")
    mirror_pre = mirrored(far_pre)
    known_partner = lax.ppermute(known, "section", [(k, (k + ring) % count) for k in range(count)])
    held = [jnp.stack([known, known_partner])]
    for steps in range(1, ring):
        held.append(inside_half(held[0], steps, ring))
    kept, sent = first_parts(spot, top, row_weight, head, known, mirror_pre, place, chips)
    received = from_other_core(sent)
    merged = added(kept, received)
    firsts = [merged[0]]
    for mask in range(1, chips):
        firsts.append(between_chips(merged[mask], mask))
    coupled_same = exchanged(
        jnp.broadcast_to(coupled[None], (blocks // 2,) + coupled.shape), "fsdp", groups
    )
    coupled_other = from_other_core(coupled_same)

    shared = chain(section, core, held, coupled_same, coupled_other, count)
    shared = exchanged(shared, "fsdp")
    shared, *firsts[1:6] = lax.optimization_barrier((shared, *firsts[1:6]))
    far_in = input_grads(wide, shared, step, 1, BF16)
    back_in = mirrored(far_in)
    cross = exchanged(folded(shared, blocks, units), "fsdp")
    own_in = input_grads(wide, shared, step, 0, F32)
    grad_out = output_grads(section, cross, firsts, inner_all, outer_all)
    grad_in = (own_in + back_in.astype(F32)).T
    return (grad_in[None], grad_out[None])


def solution(mesh):
    in_specs = (
        P("section", "fsdp", None),
        P("section", None, "fsdp"),
        P("section", None, "fsdp", None),
        P("section", None, "fsdp", None),
        P(None, None, "fsdp", None),
        P(),
        P(),
        P(),
        P(),
    )
    out_specs = (P("section", "fsdp", None), P("section", None, "fsdp"))
    return jax.shard_map(
        on_device, mesh=mesh, in_specs=in_specs, out_specs=out_specs, check_vma=False
    )
```

```python
import jax
import jax.numpy as jnp
from jax import lax
from jax.experimental import pallas as pl
from jax.experimental.pallas import tpu as pltpu
from jax.sharding import PartitionSpec as P


BF16 = jnp.bfloat16
F32 = jnp.float32
ROWS_OF_BOTH = (((0,), (0,)), ((), ()))
COLS_OF_BOTH = (((1,), (1,)), ((), ()))


def dot(left, right, dims=(((1,), (0,)), ((), ()))):
    return lax.dot_general(left, right, dims, preferred_element_type=F32)


LOWER_OFFSETS = (0, -3, -1, 4)
UPPER_OFFSETS = (1, 2, 3, -2)


def inside_half(value, steps, ends):
    ring = lax.axis_size("section") // 2
    pairs = []
    for base in (0, ring):
        pairs += [(base + (z + steps) % ring, base + z) for z in range(ends)]
    return lax.ppermute(value, "section", pairs)


def across(value, slot):
    ring = lax.axis_size("section") // 2
    low, high = LOWER_OFFSETS[slot], UPPER_OFFSETS[slot]
    pairs = [(ring + (z - high) % ring, ring + z) for z in range(ring)]
    if low:
        pairs += [((z + low) % ring, z) for z in range(ring)]
    return lax.ppermute(value, "section", pairs)


def mirrored(value):
    count = lax.axis_size("section")
    return lax.ppermute(value, "section", [(k, count - 1 - k) for k in range(count)])


def exchanged(parts, axis, groups=None):
    return lax.all_to_all(parts, axis, 0, 0, axis_index_groups=groups, tiled=True)


def same_core(count):
    return [list(range(core, count, 2)) for core in range(2)]


def from_other_core(value):
    count = lax.axis_size("fsdp")
    return lax.ppermute(value, "fsdp", [(f, f ^ 1) for f in range(count)])


def vmem():
    return pl.BlockSpec(memory_space=pltpu.VMEM)


def smem():
    return pl.BlockSpec(memory_space=pltpu.SMEM)


def couplings(section, in_t, out_t, partner, inner, outer, count):
    units = in_t.shape[0]
    ring = count // 2
    slots = len(inner)

    def kernel(section_ref, in_ref, out_ref, partner_ref, *refs):
        dest = refs[2 * slots]
        own = section_ref[0]
        upper = own >= ring

        def store(slot, other, as_lower):
            @pl.when(as_lower)
            def _():
                dest[slot] = dot(other[...], out_ref[...], COLS_OF_BOTH).astype(BF16)

            @pl.when(jnp.logical_not(as_lower))
            def _():
                dest[slot] = dot(in_ref[...], other[...], COLS_OF_BOTH).astype(BF16)

        for slot in range(slots):
            store(slot, refs[slot], jnp.where(upper, own - ring, own) + slot + 1 < ring)
        for slot in range(slots):
            other = refs[slots + slot]
            if LOWER_OFFSETS[slot] == 0:

                @pl.when(upper)
                def _():
                    dest[slots + slot] = dot(in_ref[...], other[...], COLS_OF_BOTH).astype(BF16)

                @pl.when(jnp.logical_not(upper))
                def _():
                    value = dot(partner_ref[...], out_ref[...], COLS_OF_BOTH)
                    dest[slots + slot] = value.astype(BF16)
            else:
                store(slots + slot, other, jnp.logical_not(upper))

    return pl.pallas_call(
        kernel,
        out_shape=jax.ShapeDtypeStruct((2 * slots, units, units), BF16),
        in_specs=[smem()] + [vmem()] * (3 + 2 * slots),
        out_specs=vmem(),
        name="couplings",
    )(section, in_t, out_t, partner, *inner, *outer)


def laid_out(down, up, blocks, step):
    half, width = down.shape
    part = width // blocks

    def kernel(down_ref, up_ref, dest):
        for b in range(step):
            dest[b, :half] = down_ref[:, b * part : (b + 1) * part]
            dest[b, half:] = up_ref[:, b * part : (b + 1) * part]

    return pl.pallas_call(
        kernel,
        grid=(blocks // step,),
        out_shape=jax.ShapeDtypeStruct((blocks, 2 * half, part), BF16),
        in_specs=[pl.BlockSpec((half, step * part), lambda b: (0, b))] * 2,
        out_specs=pl.BlockSpec((step, 2 * half, part), lambda b: (b, 0, 0)),
        name="laid_out",
    )(down, up)


def folded(parts, copies, used):
    blocks, _, units = parts.shape

    def kernel(parts_ref, dest):
        total = parts_ref[0].astype(F32)
        for b in range(1, blocks):
            total = total + parts_ref[b].astype(F32)
        total = total.astype(BF16)
        for c in range(copies):
            dest[c] = total

    return pl.pallas_call(
        kernel,
        grid=(1,),
        out_shape=jax.ShapeDtypeStruct((copies, used, units), BF16),
        in_specs=[pl.BlockSpec((blocks, used, units), lambda b: (0, 0, 0))],
        out_specs=pl.BlockSpec((copies, used, units), lambda b: (0, 0, 0)),
        name="folded",
    )(parts)


def folded_with(parts, below, copies, lead):
    blocks, rows, units = parts.shape
    kept = rows - lead
    half = kept // 2

    def kernel(parts_ref, below_ref, coupled, known, far):
        total = parts_ref[0].astype(F32)
        for b in range(1, blocks):
            total = total + parts_ref[b].astype(F32)
        total = total.astype(BF16)
        for c in range(copies):
            coupled[c] = total[:lead]
        known[:kept] = total[lead:]
        known[kept:] = below_ref[...]
        far[...] = total[lead + half :]

    return pl.pallas_call(
        kernel,
        out_shape=[
            jax.ShapeDtypeStruct((copies, lead, units), BF16),
            jax.ShapeDtypeStruct((kept + below.shape[0], units), BF16),
            jax.ShapeDtypeStruct((half, units), BF16),
        ],
        in_specs=[vmem(), vmem()],
        out_specs=[vmem(), vmem(), vmem()],
        name="folded_with",
    )(parts, below)


def row_setup(fsdp, plan, reward_pos, reward_cot, row_count):
    directions, micro = plan.shape
    rows = directions * micro * row_count

    def kernel(fsdp_ref, plan_ref, pos_ref, cot_ref, weight, place):
        at = fsdp_ref[0]
        row = lax.broadcasted_iota(jnp.int32, (row_count, 128), 0)
        wide_row = lax.broadcasted_iota(jnp.int32, (row_count, rows), 0)
        wide_col = lax.broadcasted_iota(jnp.int32, (row_count, rows), 1)
        for d in range(directions):
            for j in range(micro):
                ident = plan_ref[d, j]
                base = (d * micro + j) * row_count
                spot = (d * micro + ident) * row_count
                value = jnp.where(row == pos_ref[d, ident, at], cot_ref[d, ident, at], 0.0)
                weight[base : base + row_count] = value
                place[base : base + row_count] = jnp.where(
                    wide_col == wide_row + spot, 1.0, 0.0
                )

    return pl.pallas_call(
        kernel,
        out_shape=[
            jax.ShapeDtypeStruct((rows, 128), F32),
            jax.ShapeDtypeStruct((rows, rows), F32),
        ],
        in_specs=[smem()] * 4,
        out_specs=[vmem(), vmem()],
        name="row_setup",
    )(fsdp, plan, reward_pos, reward_cot)


def pre_parts(wide, coupled, in_t, far_in_t, step):
    blocks, rows, part = wide.shape
    units = in_t.shape[0]
    lead = coupled.shape[1]
    half = rows // 2

    def kernel(wide_ref, coupled_ref, in_ref, far_ref, dest):
        for b in range(step):
            dest[b, :lead] = coupled_ref[b]
            dest[b, lead : lead + half] = dot(
                wide_ref[b, :half], in_ref[...], COLS_OF_BOTH
            ).astype(BF16)
            dest[b, lead + half :] = dot(
                wide_ref[b, half:], far_ref[...], COLS_OF_BOTH
            ).astype(BF16)

    return pl.pallas_call(
        kernel,
        grid=(blocks // step,),
        out_shape=jax.ShapeDtypeStruct((blocks, lead + rows, units), BF16),
        in_specs=[
            pl.BlockSpec((step, rows, part), lambda b: (b, 0, 0)),
            pl.BlockSpec((step, lead, units), lambda b: (b, 0, 0)),
            pl.BlockSpec((units, part), lambda b: (0, 0)),
            pl.BlockSpec((units, part), lambda b: (0, 0)),
        ],
        out_specs=pl.BlockSpec((step, lead + rows, units), lambda b: (b, 0, 0)),
        name="pre_parts",
    )(wide, coupled, in_t, far_in_t)


def top_products(top, row_weight, head, out_full, place, step):
    blocks, units, part = out_full.shape
    rows = top.shape[0]

    def kernel(top_ref, weight_ref, head_ref, out_ref, place_ref, dest, acc):
        at = pl.program_id(0)

        @pl.when(at == 0)
        def _():
            acc[...] = jnp.zeros_like(acc)

        first = top_ref[...].astype(F32) + weight_ref[:, :1] * head_ref[...]
        first = first.astype(BF16)
        total = acc[...]
        for b in range(step):
            total = total + dot(first[:, b * part : (b + 1) * part], out_ref[b], COLS_OF_BOTH)
        acc[...] = total

        @pl.when(at == pl.num_programs(0) - 1)
        def _():
            dest[...] = dot(
                place_ref[...].astype(BF16), acc[...].astype(BF16), ROWS_OF_BOTH
            ).astype(BF16)

    return pl.pallas_call(
        kernel,
        grid=(blocks // step,),
        out_shape=jax.ShapeDtypeStruct((rows, units), BF16),
        in_specs=[
            pl.BlockSpec((rows, step * part), lambda b: (0, b)),
            pl.BlockSpec((rows, 128), lambda b: (0, 0)),
            pl.BlockSpec((1, step * part), lambda b: (0, b)),
            pl.BlockSpec((step, units, part), lambda b: (b, 0, 0)),
            pl.BlockSpec((rows, rows), lambda b: (0, 0)),
        ],
        out_specs=pl.BlockSpec((rows, units), lambda b: (0, 0)),
        scratch_shapes=[pltpu.VMEM((rows, units), F32)],
        name="top_products",
    )(top, row_weight, head, out_full, place)


def first_parts(top, row_weight, head, pre_down, pre_up, place, blocks, step):
    rows, width = top.shape
    half, units = pre_up.shape
    part = width // blocks

    def kernel(top_ref, weight_ref, head_ref, down_ref, up_ref, place_ref, dest):
        value = jnp.concatenate([down_ref[:half], up_ref[...]], axis=0).astype(F32)
        hidden = (value * jax.nn.sigmoid(value)).astype(BF16)
        placed = dot(place_ref[...].astype(BF16), hidden).astype(BF16)
        first = top_ref[...].astype(F32) + weight_ref[:, :1] * head_ref[...]
        first = first.astype(BF16)
        total = dot(placed, first, ROWS_OF_BOTH).astype(BF16)
        for b in range(step):
            dest[b] = total[:, b * part : (b + 1) * part]

    return pl.pallas_call(
        kernel,
        grid=(blocks // step,),
        out_shape=jax.ShapeDtypeStruct((blocks, units, part), BF16),
        in_specs=[
            pl.BlockSpec((rows, step * part), lambda b: (0, b)),
            pl.BlockSpec((rows, 128), lambda b: (0, 0)),
            pl.BlockSpec((1, step * part), lambda b: (0, b)),
            pl.BlockSpec((2 * rows, units), lambda b: (0, 0)),
            pl.BlockSpec((half, units), lambda b: (0, 0)),
            pl.BlockSpec((rows, rows), lambda b: (0, 0)),
        ],
        out_specs=pl.BlockSpec((step, units, part), lambda b: (b, 0, 0)),
        name="first_parts",
    )(top, row_weight, head, pre_down, pre_up, place)


def held_at(upper, lower, count):
    ring = count // 2
    if upper // ring == lower // ring:
        gap = upper - lower
        return (lower, gap - 1) if gap <= ring // 2 else (upper, ring - gap - 1)
    gap = (upper - lower) % ring
    for slot in range(ring // 2):
        if LOWER_OFFSETS[slot] % ring == gap:
            return lower, ring // 2 + slot
        if UPPER_OFFSETS[slot] % ring == gap:
            return upper, ring // 2 + slot


def chain(section, core, held, same, other, count):
    ring = count // 2
    _, tall, units = held[0].shape
    rows = tall // 2
    half = rows // 2

    def kernel(section_ref, core_ref, same_ref, other_ref, *refs):
        dest, known_ref, reach, grads = refs[ring:]
        even = core_ref[0] == 0
        own = section_ref[0]
        base = jnp.where(own >= ring, ring, 0)
        for steps in range(ring):
            at = lax.rem(own - base + steps, ring)
            known_ref[base + at] = refs[steps][0]
            known_ref[ring - base + at] = refs[steps][1]

        def pre_of(layer, other):
            return jnp.concatenate(
                [
                    known_ref[layer, :half],
                    known_ref[other, half:rows],
                ],
                axis=0,
            ).astype(F32)

        def coupling(upper, lower):
            at, slot = held_at(upper, lower, count)
            mine, theirs = same_ref[slot, at], other_ref[slot, at]
            return jnp.concatenate(
                [jnp.where(even, mine, theirs), jnp.where(even, theirs, mine)], axis=0
            )

        for layer in range(count):
            reach[layer] = known_ref[layer, rows:].astype(F32)
        for layer in range(count - 1, -1, -1):
            pre = pre_of(layer, count - 1 - layer)
            sig = jax.nn.sigmoid(pre)
            grad_pre = (reach[layer] * sig * (1.0 + pre * (1.0 - sig))).astype(BF16)
            grads[layer] = grad_pre
            if layer > 0:
                lower = jnp.concatenate([coupling(layer, low) for low in range(layer)], axis=1)
                update = dot(grad_pre, lower)
                for low in range(layer):
                    reach[low] += update[:, low * units : (low + 1) * units]
        far = count - 1 - own
        pre = pre_of(own, far)
        hidden = (pre * jax.nn.sigmoid(pre)).astype(BF16)
        above = jnp.concatenate(
            [grads[jnp.minimum(own + up, count - 1)] for up in range(1, count)], axis=1
        )
        cross = dot(hidden, above, ROWS_OF_BOTH)
        sent = jnp.concatenate([grads[own][:half], grads[far][half:]], axis=0)
        for up in range(count):
            if up == 0:
                dest[up, :units] = jnp.zeros((units, units), BF16)
            else:
                block = cross[:, (up - 1) * units : up * units]
                dest[up, :units] = jnp.where(own + up < count, block, 0.0).astype(BF16)
            dest[up, units:] = sent

    return pl.pallas_call(
        kernel,
        out_shape=jax.ShapeDtypeStruct((count, units + rows, units), BF16),
        in_specs=[smem(), smem()] + [vmem()] * (2 + ring),
        out_specs=vmem(),
        scratch_shapes=[
            pltpu.VMEM((count, tall, units), BF16),
            pltpu.VMEM((count, rows, units), F32),
            pltpu.VMEM((count, rows, units), BF16),
        ],
        name="chain",
    )(section, core, same, other, *held)


def input_grads(wide, shared, step, side, kind):
    blocks, rows, part = wide.shape
    tall, units = shared.shape[1:]
    half = rows // 2
    skip = tall - rows + side * half

    def kernel(wide_ref, shared_ref, dest, acc):
        at = pl.program_id(0)

        @pl.when(at == 0)
        def _():
            acc[...] = jnp.zeros_like(acc)

        total = acc[...]
        for b in range(step):
            total = total + dot(shared_ref[b, skip : skip + half], wide_ref[b], ROWS_OF_BOTH)
        acc[...] = total

        @pl.when(at == pl.num_programs(0) - 1)
        def _():
            dest[...] = acc[...].astype(kind)

    return pl.pallas_call(
        kernel,
        grid=(blocks // step,),
        out_shape=jax.ShapeDtypeStruct((units, part), kind),
        in_specs=[
            pl.BlockSpec((step, half, part), lambda b: (b, side, 0)),
            pl.BlockSpec((step, tall, units), lambda b: (b, 0, 0)),
        ],
        out_specs=pl.BlockSpec((units, part), lambda b: (0, 0)),
        scratch_shapes=[pltpu.VMEM((units, part), F32)],
    )(wide, shared)


def output_grads(section, cross, first, weights):
    count, units, _ = cross.shape
    part = first.shape[1]
    ring = count // 2

    def kernel(section_ref, cross_ref, first_ref, weights_ref, dest):
        own = section_ref[0]
        upper = own >= ring
        place = jnp.where(upper, own - ring, own)
        dest[...] = first_ref[...].astype(F32)
        for z in range(ring):

            @pl.when(z > place)
            def _():
                dest[...] += dot(cross_ref[z - place], weights_ref[z, 0])

            @pl.when(jnp.logical_not(upper))
            def _():
                dest[...] += dot(cross_ref[jnp.minimum(ring + z - place, count - 1)], weights_ref[z, 1])

    return pl.pallas_call(
        kernel,
        out_shape=jax.ShapeDtypeStruct((units, part), F32),
        in_specs=[smem()] + [vmem()] * 3,
        out_specs=vmem(),
        name="output_grads",
    )(section, cross, first, weights)


def on_device(
    branch_in,
    branch_out,
    down_inputs,
    up_inputs,
    top_grads,
    plan,
    reward_pos,
    reward_cot,
    reward_head,
):
    count = lax.axis_size("section")
    blocks = lax.axis_size("fsdp")
    section_idx = lax.axis_index("section")
    fsdp_idx = lax.axis_index("fsdp")
    section = section_idx.astype(jnp.int32).reshape(1)
    _, micro, row_count, width = down_inputs.shape
    units = branch_in.shape[2]
    part = width // blocks
    half = micro * row_count
    rows = 2 * half
    step = 4

    core = (fsdp_idx % 2).astype(jnp.int32).reshape(1)
    groups = same_core(blocks)

    in_t = branch_in[0].T
    out_t = branch_out[0]
    down = down_inputs[0].reshape(half, width)
    up = up_inputs[0].reshape(half, width)
    out_full = lax.all_gather(out_t, "fsdp", axis=0)
    wide = exchanged(laid_out(down, up, blocks, step), "fsdp")
    ring = count // 2
    place_idx = section_idx % ring
    partner = lax.ppermute(
        jnp.where(section_idx >= ring, in_t, out_t),
        "section",
        [(k, (k + ring) % count) for k in range(count)],
    )
    inner, outer = [], []
    for slot in range(ring // 2):
        steps = slot + 1
        inner.append(
            inside_half(
                jnp.where(place_idx >= steps, in_t, out_t),
                steps,
                ring // 2 if 2 * steps == ring else ring,
            )
        )
    far_in_t = mirrored(in_t)
    for slot in range(ring // 2):
        outer.append(across(partner, slot))
    weights = lax.all_gather(
        jnp.stack([in_t, partner]),
        "section",
        axis=0,
        axis_index_groups=[list(range(ring)), list(range(ring, count))],
    )

    coupled = couplings(section, in_t, out_t, partner, inner, outer, count)
    coupled = coupled.reshape(blocks, -1, units)
    lead = coupled.shape[1]
    row_weight, place = row_setup(
        fsdp_idx.astype(jnp.int32).reshape(1), plan, reward_pos, reward_cot, row_count
    )
    top = top_grads.reshape(rows, width)
    head = reward_head.reshape(1, width)
    parts = pre_parts(wide, coupled, in_t, far_in_t, step)
    parts = exchanged(parts, "fsdp")
    reached = top_products(top, row_weight, head, out_full, place, step)
    coupled, known, far_pre = folded_with(parts, reached, count, lead)
    coupled = exchanged(coupled, "section")
    mirror_pre = mirrored(far_pre)
    known_partner = lax.ppermute(known, "section", [(k, (k + ring) % count) for k in range(count)])
    held = [jnp.stack([known, known_partner])]
    for steps in range(1, ring):
        held.append(inside_half(held[0], steps, ring))
    firsts = first_parts(top, row_weight, head, known, mirror_pre, place, blocks, step)
    first = lax.psum_scatter(
        firsts.reshape(blocks * units, part), "fsdp", scatter_dimension=0, tiled=True
    )
    coupled_same = exchanged(
        jnp.broadcast_to(coupled[None], (blocks // 2,) + coupled.shape), "fsdp", groups
    )
    coupled_other = from_other_core(coupled_same)

    shared = chain(section, core, held, coupled_same, coupled_other, count)
    shared = exchanged(shared, "fsdp")
    far_in = input_grads(wide, shared, step, 1, BF16)
    back_in = mirrored(far_in)
    cross = exchanged(folded(shared, blocks, units), "fsdp")
    own_in = input_grads(wide, shared, step, 0, F32)
    grad_out = output_grads(section, cross, first, weights)
    grad_in = (own_in + back_in.astype(F32)).T
    return (grad_in[None], grad_out[None])


def solution(mesh):
    in_specs = (
        P("section", "fsdp", None),
        P("section", None, "fsdp"),
        P("section", None, "fsdp", None),
        P("section", None, "fsdp", None),
        P(None, None, "fsdp", None),
        P(),
        P(),
        P(),
        P(),
    )
    out_specs = (P("section", "fsdp", None), P("section", None, "fsdp"))
    return jax.shard_map(
        on_device, mesh=mesh, in_specs=in_specs, out_specs=out_specs, check_vma=False
    )
```
